256 devices in a mesh: ctx: 64 (over x, y_hi, z), tp: 4 (over y_lo, core).
Axes of the slice: x: 4, y: 4 (y_hi: 2, y_lo: 2; y = y_hi * 2 + y_lo), z: 8, core: 2. Of those that a mesh axis runs over, the one named last changes fastest.
Arguments:
- queries: bfloat16 [16384, 2048], P('ctx', 'tp'), may hold values from -6 to 6
- keys: bfloat16 [16384, 2048], P('ctx', 'tp'), may hold values from -6 to 6
- values: bfloat16 [16384, 2048], P('ctx', 'tp'), may hold values from -6 to 6
- out_grad: bfloat16 [16384, 4096], P('ctx', 'tp'), may hold values from -6 to 6
- w_out: bfloat16 [2048, 4096], P('tp'), may hold values from -0.09375 to 0.09375
- offsets: int32 [16, 3], P('tp'), may hold values from 0 to 3, as said below
Outputs:
- query_grad: bfloat16 [16384, 2048], P('ctx', 'tp')
- key_grad: bfloat16 [16384, 2048], P('ctx', 'tp')
- value_grad: bfloat16 [16384, 2048], P('ctx', 'tp')
The draws below stay inside these ranges and needn't reach their ends.
Inputs may be any that keep to these rules, and one draw needn't show every extreme that they name: offsets[h, l] lies between 0 and 2^l - 1.
All inputs are finite; a program needn't handle non-finite values.
Results may differ from the reference program's by a relative error of at most 0.017.
Values may be sent and summed in bfloat16 or wider, within the bound.
No kernel may reach another device: no remote copies, remote signals or barrier semaphores. Data moves between devices by JAX's collectives and lax.ppermute only.
A program may use at most 64 MiB of HBM per device.

```python
import math
import jax
import jax.numpy as jnp
from jax import lax

D = 4096
HEADS = 16
HEAD_DIM = 128
LEVELS = 3
TOK_DEV = 256
TOKENS = 16384
KEYS_SEG = 1024


def draw_queries(key, part):
    drawn = jax.random.normal(jax.random.fold_in(key, 1), (TOKENS, HEADS * HEAD_DIM), jnp.float32)
    return jnp.clip(drawn, -6.0, 6.0).astype(jnp.bfloat16)


def draw_keys(key, part):
    drawn = jax.random.normal(jax.random.fold_in(key, 2), (TOKENS, HEADS * HEAD_DIM), jnp.float32)
    return jnp.clip(drawn, -6.0, 6.0).astype(jnp.bfloat16)


def draw_offsets(key, part):
    columns = []
    for level_num in range(LEVELS):
        order = jax.random.permutation(jax.random.fold_in(key, 11 + level_num), HEADS)
        columns.append(2 ** level_num - 1 - order * 2 ** level_num // HEADS)
    return jnp.stack(columns, axis=1).astype(jnp.int32)


def shard_levels(rng, extent, pieces, smallest, high):
    level, own = 1.0, jax.random.fold_in(rng, 6)
    for axis_at, parts in pieces:
        heights = jnp.exp(jax.random.uniform(jax.random.fold_in(own, axis_at), (parts,), jnp.float32, smallest / len(pieces), high / len(pieces)))
        level = level * jnp.repeat(heights, extent[axis_at] // parts).reshape([-1 if axis == axis_at else 1 for axis in range(len(extent))])
    return level


def scatter_about(key, shape, scale, bound, cuts=(), held_as=jnp.bfloat16):
    values = scale * jax.random.normal(key, shape, jnp.float32)
    if cuts:
        values = values * shard_levels(key, shape, cuts, -0.22, 0.18)
    return jnp.clip(values, -bound, bound).astype(held_as)


def setup_inputs(seed: int = 0) -> dict:
    seeds = jax.random.split(jax.random.key(seed), 7)
    queries = draw_queries(jax.random.fold_in(seeds[6], 71), 0)
    keys = draw_keys(jax.random.fold_in(seeds[6], 71), 0)
    values = scatter_about(seeds[2], (TOKENS, HEADS * HEAD_DIM), 1.0, 6.0, ((0, 64), (1, 4)))
    out_grad = scatter_about(seeds[3], (TOKENS, D), 1.0, 6.0, ((0, 64), (1, 4)))
    w_out = scatter_about(seeds[4], (HEADS * HEAD_DIM, D), D ** -0.5, 0.09375, ((0, 4),))
    offsets = draw_offsets(jax.random.fold_in(seeds[6], 71), 0)
    return dict(queries=queries, keys=keys, values=values, out_grad=out_grad, w_out=w_out, offsets=offsets)


NEGATIVE_FILL = -1e+30
HIGHEST_PRECISION = lax.Precision.HIGHEST

def low_round(values_in):
    return lax.optimization_barrier(values_in.astype(jnp.bfloat16)).astype(jnp.float32)

def reference(queries, keys, values, out_grad, w_out, offsets):
    score_scale = 1.0 / math.sqrt(HEAD_DIM)
    rotation = 2 * TOK_DEV
    grad_full = jnp.dot(out_grad, w_out.T, preferred_element_type=jnp.float32).astype(jnp.bfloat16)
    queries = jnp.roll(queries, -rotation, axis=0)
    keys = jnp.roll(keys, -rotation, axis=0)
    values = jnp.roll(values, -rotation, axis=0)
    grad_out = jnp.roll(grad_full, -rotation, axis=0)
    query_cols, key_cols, value_cols = ([], [], [])
    for head_num in range(HEADS):
        first_col = head_num * HEAD_DIM
        query_head = queries[:, first_col:first_col + HEAD_DIM].astype(jnp.float32)
        key_head = keys[:, first_col:first_col + HEAD_DIM].astype(jnp.float32)
        value_head = values[:, first_col:first_col + HEAD_DIM].astype(jnp.float32)
        grad_head = grad_out[:, first_col:first_col + HEAD_DIM].astype(jnp.float32)
        saved, tops, totals, sums = ([], [], [], [])
        for level_num in range(LEVELS):
            stride = 2 ** level_num
            seg_rows = min(KEYS_SEG, TOKENS // stride)
            causal = jnp.tril(jnp.ones((seg_rows, seg_rows), dtype=bool))
            positions = (offsets[head_num, level_num] + stride * jnp.arange(TOKENS // stride, dtype=jnp.int32)).astype(jnp.int32)
            query_pack = jnp.take(query_head, positions, axis=0).reshape(-1, seg_rows, HEAD_DIM)
            key_pack = jnp.take(key_head, positions, axis=0).reshape(-1, seg_rows, HEAD_DIM)
            value_pack = jnp.take(value_head, positions, axis=0).reshape(-1, seg_rows, HEAD_DIM)
            grad_pack = jnp.take(grad_head, positions, axis=0).reshape(-1, seg_rows, HEAD_DIM)
            scores = jnp.einsum('sad,sbd->sab', query_pack, key_pack, precision=HIGHEST_PRECISION) * score_scale
            scores = jnp.where(causal, scores, NEGATIVE_FILL)
            row_top = lax.optimization_barrier(jnp.max(scores, axis=2))
            weights = jnp.where(causal, jnp.exp(scores - row_top[:, :, None]), 0.0)
            level_sum = jnp.einsum('sab,sbd->sad', weights, value_pack, precision=HIGHEST_PRECISION)
            tops.append(jnp.full((TOKENS,), NEGATIVE_FILL, jnp.float32).at[positions].set(row_top.reshape(-1)))
            totals.append(jnp.zeros((TOKENS,), jnp.float32).at[positions].set(lax.optimization_barrier(jnp.sum(weights, axis=2)).reshape(-1)))
            sums.append(jnp.zeros((TOKENS, HEAD_DIM), jnp.float32).at[positions].set(level_sum.reshape(-1, HEAD_DIM)))
            saved.append((positions, causal, seg_rows, scores, query_pack, key_pack, value_pack, grad_pack))
        row_top = tops[0]
        for level_top in tops[1:]:
            row_top = jnp.maximum(row_top, level_top)
        row_total = jnp.zeros((TOKENS,), jnp.float32)
        out_sum = jnp.zeros((TOKENS, HEAD_DIM), jnp.float32)
        for level_top, level_total, level_sum in zip(tops, totals, sums):
            factor = jnp.exp(level_top - row_top)
            row_total = row_total + level_total * factor
            out_sum = out_sum + level_sum * factor[:, None]
        log_total = row_top + jnp.log(row_total)
        attn_out = out_sum / row_total[:, None]
        delta = lax.optimization_barrier(jnp.sum(grad_head * attn_out, axis=1))
        query_grad = jnp.zeros((TOKENS, HEAD_DIM), jnp.float32)
        key_grad = jnp.zeros((TOKENS, HEAD_DIM), jnp.float32)
        value_grad = jnp.zeros((TOKENS, HEAD_DIM), jnp.float32)
        for positions, causal, seg_rows, scores, query_pack, key_pack, value_pack, grad_pack in saved:
            log_pack = jnp.take(log_total, positions).reshape(-1, seg_rows)
            delta_pack = jnp.take(delta, positions).reshape(-1, seg_rows)
            weight = jnp.where(causal, jnp.exp(scores - log_pack[:, :, None]), 0.0)
            prob_grad = jnp.einsum('sad,sbd->sab', grad_pack, value_pack, precision=HIGHEST_PRECISION)
            score_grad = low_round(weight * (prob_grad - delta_pack[:, :, None]))
            weight_low = low_round(weight)
            query_grad = query_grad.at[positions].add(jnp.einsum('sab,sbd->sad', score_grad, key_pack, precision=HIGHEST_PRECISION).reshape(-1, HEAD_DIM))
            key_grad = key_grad.at[positions].add(jnp.einsum('sab,sad->sbd', score_grad, query_pack, precision=HIGHEST_PRECISION).reshape(-1, HEAD_DIM))
            value_grad = value_grad.at[positions].add(jnp.einsum('sab,sad->sbd', weight_low, grad_pack, precision=HIGHEST_PRECISION).reshape(-1, HEAD_DIM))
        query_cols.append(jnp.roll((query_grad * score_scale).astype(jnp.bfloat16), rotation, axis=0))
        key_cols.append(jnp.roll((key_grad * score_scale).astype(jnp.bfloat16), rotation, axis=0))
        value_cols.append(jnp.roll(value_grad.astype(jnp.bfloat16), rotation, axis=0))
    return (jnp.concatenate(query_cols, axis=1), jnp.concatenate(key_cols, axis=1), jnp.concatenate(value_cols, axis=1))
```

```python
import functools
import math

import jax
import jax.numpy as jnp
from jax import lax
from jax.experimental import pallas as pl
from jax.experimental.pallas import tpu as pltpu
from jax.sharding import PartitionSpec as P

TOK = 256
DIM = 128
BLOCK = 4 * TOK
SCALE = 1.0 / math.sqrt(DIM)
SCALE2 = SCALE * math.log2(math.e)
NEG = -1e30
F32 = jnp.float32
BF16 = jnp.bfloat16


def token_of_row(row):
    return 4 * (row & 63) + 2 * ((row >> 6) & 1) + (row >> 7)


def token_of_row_1(row):
    return 4 * (row & 63) + 2 * (row >> 6)


def iota(shape, dim):
    return lax.broadcasted_iota(jnp.int32, shape, dim)


def dot_nt(a, b):
    return lax.dot_general(a, b, (((1,), (1,)), ((), ())), preferred_element_type=F32)


def dot_nn(a, b):
    return lax.dot_general(a, b, (((1,), (0,)), ((), ())), preferred_element_type=F32)


def dot_tn(a, b):
    return lax.dot_general(a, b, (((0,), (0,)), ((), ())), preferred_element_type=F32)


def rows_at(start, size, unit=64):
    return pl.ds(pl.multiple_of(start, unit), size)


def cols_at(head):
    return pl.ds(pl.multiple_of(head * DIM, DIM), DIM)


def sort_matrix():
    return (iota((TOK, TOK), 1) == token_of_row(iota((TOK, TOK), 0))).astype(BF16)


def unsort_matrix():
    return (iota((TOK, TOK), 0) == token_of_row(iota((TOK, TOK), 1))).astype(BF16)


def wide_max(scores):
    return jnp.broadcast_to(jnp.max(scores, axis=1, keepdims=True), (scores.shape[0], DIM))


def call(kernel, outs, scratch=(), name=None, flops=0, bytes_accessed=0):
    def run(meta, *args):
        return pl.pallas_call(
            kernel,
            out_shape=[jax.ShapeDtypeStruct(shape, dtype) for shape, dtype in outs],
            in_specs=[pl.BlockSpec(memory_space=pltpu.SMEM)]
            + [pl.BlockSpec(memory_space=pltpu.VMEM)] * len(args),
            out_specs=[pl.BlockSpec(memory_space=pltpu.VMEM)] * len(outs),
            scratch_shapes=list(scratch),
            compiler_params=pltpu.CompilerParams(vmem_limit_bytes=40 << 20),
            cost_estimate=pl.CostEstimate(
                flops=flops, bytes_accessed=bytes_accessed, transcendentals=0
            ),
            name=name,
        )(meta, *args)

    return run


def pack_kernel(meta, q, k, v, *outs):
    kvs, qs = outs[:4], outs[4:]
    sort = sort_matrix()
    for s in range(4):
        head = (meta[0] + s) & 3
        kvs[s][:TOK] = dot_nn(sort, k[:, cols_at(head)]).astype(BF16)
        kvs[s][TOK:] = dot_nn(sort, v[:, cols_at(head)]).astype(BF16)
        qs[s][...] = dot_nn(sort, q[:, cols_at(head)]).astype(BF16)


def gather_kernel(meta, p0, p1, p2, p3, kv, kv1, kv2):
    for s, piece in enumerate((p0, p1, p2, p3)):
        place = (meta[0] - s) & 3
        for part in range(2):
            own = piece.at[part * TOK : (part + 1) * TOK]
            kv[rows_at(part * BLOCK + place * TOK, TOK)] = own[...]
            kv1[rows_at(part * 512 + place * 128, 128)] = own[rows_at(meta[2] * 128, 128)]
            kv2[rows_at(part * 256 + place * 64, 64)] = own[rows_at(meta[3] * 64, 64)]


def grad_kernel(meta, g0, g1, g2, g3, w, *outs):
    tp = meta[4]
    total = None
    for m, part in enumerate((g0, g1, g2, g3)):
        width = part.shape[1]
        cols = pl.ds(pl.multiple_of((tp ^ m) * width, width), width)
        term = dot_nt(part[...], w[:, cols])
        total = term if total is None else total + term
    sort = sort_matrix()
    sorted_grad = outs[4]
    sorted_grad[...] = dot_nn(sort, total.astype(BF16)).astype(BF16)
    for s in range(4):
        outs[s][...] = sorted_grad[:, cols_at((meta[0] + s) & 3)]


def ones_beside(target, values):
    target[:, :DIM] = values
    target[:, DIM:] = jnp.ones((target.shape[0], DIM), BF16)


def own_forward_kernel(
    meta, q0, q1, q2, q3, kv, kv1, kv2, qa, e0, e1, e2, top, out, vx0, vx1, vx2
):
    off1, group2 = meta[2], meta[3]
    for s, piece in enumerate((q0, q1, q2, q3)):
        qa[rows_at(((meta[0] - s) & 3) * TOK, TOK)] = piece[...]
    ones_beside(vx0, kv[BLOCK:])
    ones_beside(vx1, kv1[512:])
    ones_beside(vx2, kv2[256:])
    mask0 = token_of_row(iota((256, 256), 1)) <= token_of_row(iota((256, 256), 0))
    mask1 = token_of_row_1(iota((128, 128), 1)) <= token_of_row_1(iota((128, 128), 0))
    for b in range(4):
        strip = slice(b * 256, (b + 1) * 256)
        rows1 = rows_at(b * 256 + off1 * 128, 128)
        rows2 = rows_at(b * 256 + group2 * 64, 64)
        d1 = slice(b * 128, (b + 1) * 128)
        d2 = slice(b * 64, (b + 1) * 64)
        query, query1, query2 = qa[strip], qa[rows1], qa[rows2]
        near0 = jnp.where(mask0, dot_nt(query, kv[strip]) * SCALE2, NEG)
        near1 = jnp.where(mask1, dot_nt(query1, kv1[d1]) * SCALE2, NEG)
        mask2 = iota((64, 256), 1) <= iota((64, 256), 0) + b * 64
        all2 = jnp.where(mask2, dot_nt(query2, kv2[:256]) * SCALE2, NEG)
        high = wide_max(near0)
        high1 = wide_max(near1)
        if b:
            far0 = dot_nt(query, kv[: b * 256]) * SCALE2
            far1 = dot_nt(query1, kv1[: b * 128]) * SCALE2
            high = jnp.maximum(high, wide_max(far0))
            high1 = jnp.maximum(high1, wide_max(far1))
        top[strip] = high
        top[rows1] = jnp.maximum(top[rows1], high1)
        top[rows2] = jnp.maximum(top[rows2], wide_max(all2))
        top0, top1, top2 = top[strip][:, :1], top[rows1][:, :1], top[rows2][:, :1]
        w = jnp.exp2(near0 - top0).astype(BF16)
        e0[strip, strip] = w
        total = dot_nn(w, vx0[strip])
        if b:
            w = jnp.exp2(far0 - top0).astype(BF16)
            e0[strip, : b * 256] = w
            total = total + dot_nn(w, vx0[: b * 256])
        out[strip] = total
        w = jnp.exp2(near1 - top1).astype(BF16)
        e1[d1, d1] = w
        total = dot_nn(w, vx1[d1])
        if b:
            w = jnp.exp2(far1 - top1).astype(BF16)
            e1[d1, : b * 128] = w
            total = total + dot_nn(w, vx1[: b * 128])
        out[rows1] += total
        w = jnp.exp2(all2 - top2).astype(BF16)
        e2[d2] = w
        out[rows2] += dot_nn(w, vx2[...])


def cross_kernel(
    meta, qa, x1, x21, x22, x23, top, out, p0, p1, p2, p3,
    doa, dq, factor, delta, g1, g21, g22, g23,
    pq1, pq2, pd1, pd2, sc1, sc2, e1, e2, newtop, newout, inv, vx1, vx2,
):
    block, off1, group2 = meta[1], meta[2], meta[3]
    second = (block & 1) == 1
    earlier = ((x21, g21), (x22, g22), (x23, g23))
    for s, piece in enumerate((p0, p1, p2, p3)):
        doa[rows_at(((meta[0] - s) & 3) * TOK, TOK)] = piece[...]
    where1 = [rows_at(b * 256 + off1 * 128, 128) for b in range(4)]
    where2 = [rows_at(b * 256 + group2 * 64, 64) for b in range(4)]
    for b in range(4):
        pq1[b * 128 : (b + 1) * 128] = qa[where1[b]]
        pq2[b * 64 : (b + 1) * 64] = qa[where2[b]]
    newtop[...] = top[...]

    @pl.when(second)
    def _():
        ones_beside(vx1, x1[512:])
        sc1[...] = dot_nt(pq1[...], x1[:512]) * SCALE2
        for b in range(4):
            high = wide_max(sc1[b * 128 : (b + 1) * 128])
            newtop[where1[b]] = jnp.maximum(newtop[where1[b]], high)

    for d, (x2, _) in enumerate(earlier):

        @pl.when(block > d)
        def _(d=d, x2=x2):
            ones_beside(vx2.at[d], x2[256:])
            sc2[d] = dot_nt(pq2[...], x2[:256]) * SCALE2
            for b in range(4):
                high = wide_max(sc2[d, b * 64 : (b + 1) * 64])
                newtop[where2[b]] = jnp.maximum(newtop[where2[b]], high)

    shrink = jnp.exp2(top[...] - newtop[...])
    newout[:, :DIM] = out[:, :DIM] * shrink
    newout[:, DIM:] = out[:, DIM:] * shrink

    @pl.when(second)
    def _():
        for b in range(4):
            part = slice(b * 128, (b + 1) * 128)
            w = jnp.exp2(sc1[part] - newtop[where1[b]][:, :1]).astype(BF16)
            e1[part] = w
            newout[where1[b]] += dot_nn(w, vx1[...])

    for d in range(3):

        @pl.when(block > d)
        def _(d=d):
            for b in range(4):
                part = slice(b * 64, (b + 1) * 64)
                w = jnp.exp2(sc2[d, part] - newtop[where2[b]][:, :1]).astype(BF16)
                e2[d, part] = w
                newout[where2[b]] += dot_nn(w, vx2[d])

    inv[...] = 1.0 / newout[:, DIM:]
    grads = doa[...].astype(F32)
    row_delta = jnp.sum(grads * newout[:, :DIM] * inv[...], axis=1, keepdims=True)
    delta[...] = jnp.broadcast_to(row_delta, delta.shape)
    factor[...] = shrink * inv[...]
    dq[...] = jnp.zeros(dq.shape, F32)
    for b in range(4):
        pd1[b * 128 : (b + 1) * 128] = (doa[where1[b]].astype(F32) * inv[where1[b]]).astype(BF16)
        pd2[b * 64 : (b + 1) * 64] = (doa[where2[b]].astype(F32) * inv[where2[b]]).astype(BF16)

    @pl.when(second)
    def _():
        prob = dot_nt(pd1[...], x1[512:])
        level = jnp.concatenate([(delta[r] * inv[r])[:, :1] for r in where1], axis=0)
        score_grad = (e1[...].astype(F32) * (prob - level)).astype(BF16)
        part = dot_nn(score_grad, x1[:512])
        for b in range(4):
            dq[where1[b]] += part[b * 128 : (b + 1) * 128]
        g1[:512] = (dot_tn(score_grad, pq1[...]) * SCALE).astype(BF16)
        g1[512:] = dot_tn(e1[...], pd1[...]).astype(BF16)

    for d, (x2, g2) in enumerate(earlier):

        @pl.when(block > d)
        def _(d=d, x2=x2, g2=g2):
            prob = dot_nt(pd2[...], x2[256:])
            level = jnp.concatenate([(delta[r] * inv[r])[:, :1] for r in where2], axis=0)
            score_grad = (e2[d].astype(F32) * (prob - level)).astype(BF16)
            part = dot_nn(score_grad, x2[:256])
            for b in range(4):
                dq[where2[b]] += part[b * 64 : (b + 1) * 64]
            g2[:256] = (dot_tn(score_grad, pq2[...]) * SCALE).astype(BF16)
            g2[256:] = dot_tn(e2[d], pd2[...]).astype(BF16)


def own_backward_kernel(
    meta, e0, e1, e2, factor, delta, doa, qa, kv, kv1, kv2, dq_in,
    o0, o1, o2, o3, dkv, dq, low, shift, dkv1, dkv2, low_q,
):
    off1, group2 = meta[2], meta[3]
    low[...] = (doa[...].astype(F32) * factor[...]).astype(BF16)
    shift[...] = factor[...] * delta[...]
    dq[...] = dq_in[...]
    for b in range(3, -1, -1):
        strip = slice(b * 256, (b + 1) * 256)
        n0, n1 = (b + 1) * 256, (b + 1) * 128
        rows1 = rows_at(b * 256 + off1 * 128, 128)
        rows2 = rows_at(b * 256 + group2 * 64, 64)
        d1 = slice(b * 128, (b + 1) * 128)
        d2 = slice(b * 64, (b + 1) * 64)
        parts = (
            (strip, strip, e0, kv, BLOCK, n0, dkv),
            (rows1, d1, e1, kv1, 512, n1, dkv1),
            (rows2, d2, e2, kv2, 256, 256, dkv2),
        )
        for rows, part, weights, pair, half, count, grads in parts:
            grad_low = low[rows]
            prob = dot_nt(grad_low, pair[half : half + count])
            w = weights[part, :count]
            score_grad = (w.astype(F32) * (prob - shift[rows][:, :1])).astype(BF16)
            dq[rows] += dot_nn(score_grad, pair[:count])
            key_term = dot_tn(score_grad, qa[rows])
            value_term = dot_tn(w, grad_low)
            if b == 3:
                grads[:count] = key_term
                grads[half : half + count] = value_term
            else:
                grads[:count] += key_term
                grads[half : half + count] += value_term
    for p in range(4):
        for part in range(2):
            dkv[rows_at(part * BLOCK + p * 256 + off1 * 128, 128)] += dkv1[
                part * 512 + p * 128 : part * 512 + (p + 1) * 128
            ]
            dkv[rows_at(part * BLOCK + p * 256 + group2 * 64, 64)] += dkv2[
                part * 256 + p * 64 : part * 256 + (p + 1) * 64
            ]
    dkv[:BLOCK] = dkv[:BLOCK] * SCALE
    low_q[...] = (dq[...] * SCALE).astype(BF16)
    for s, target in enumerate((o0, o1, o2, o3)):
        target[...] = low_q[rows_at(((meta[0] + s) & 3) * TOK, TOK)]


def combine_kernel(meta, dkv, y1, y21, y22, y23, o0, o1, o2, o3, total):
    off1, group2 = meta[2], meta[3]
    total[...] = dkv[...]
    for p in range(4):
        for part in range(2):
            one = slice(part * 512 + p * 128, part * 512 + (p + 1) * 128)
            two = slice(part * 256 + p * 64, part * 256 + (p + 1) * 64)
            total[rows_at(part * BLOCK + p * 256 + off1 * 128, 128)] += y1[one].astype(F32)
            total[rows_at(part * BLOCK + p * 256 + group2 * 64, 64)] += (
                y21[two].astype(F32) + y22[two].astype(F32) + y23[two].astype(F32)
            )
    for s, target in enumerate((o0, o1, o2, o3)):
        place = (meta[0] + s) & 3
        for part in range(2):
            target[part * TOK : (part + 1) * TOK] = total[
                rows_at(part * BLOCK + place * TOK, TOK)
            ].astype(BF16)


def finish_kernel(meta, q0, q1, q2, q3, r0, r1, r2, r3, dq, dk, dv):
    unsort = unsort_matrix()
    for s, (query, pair) in enumerate(((q0, r0), (q1, r1), (q2, r2), (q3, r3))):
        cols = cols_at((meta[0] - s) & 3)
        dq[:, cols] = dot_nn(unsort, query[...]).astype(BF16)
        dk[:, cols] = dot_nn(unsort, pair[:TOK]).astype(BF16)
        dv[:, cols] = dot_nn(unsort, pair[TOK:]).astype(BF16)


def local(queries, keys, values, out_grad, w_out, offsets):
    devices = lax.axis_size("ctx")
    seat = (lax.axis_index("ctx") - 2) % devices
    place, block, tp = seat % 4, seat // 4 % 4, lax.axis_index("tp")
    own = lax.dynamic_slice_in_dim(offsets, place, 1, 0)[0]
    meta = jnp.stack([place, block, own[1], ((own[2] & 1) << 1) | (own[2] >> 1), tp])

    def at(index):
        return (index + 2) % devices

    def exchange(part, s):
        route = [
            (at(u), at(u // 4 * 4 + (u % 4 + s) % 4)) for u in range(devices)
        ]
        return lax.ppermute(part, "ctx", route)

    def to_block(part, distance, blocks):
        route = [
            (at(u), at(u + 4 * distance)) for u in range(devices) if u // 4 % 4 in blocks
        ]
        return lax.ppermute(part, "ctx", route)

    def across(part, m):
        return lax.ppermute(part, "tp", [(i, i ^ m) for i in range(4)])

    packed = call(
        pack_kernel, [((2 * TOK, DIM), BF16)] * 4 + [((TOK, DIM), BF16)] * 4, name="pack"
    )(meta, queries, keys, values)
    pairs = [packed[0]] + [exchange(packed[s], s) for s in (1, 2, 3)]
    grad_y = across(out_grad, 2)
    query_parts = [packed[4]] + [exchange(packed[4 + s], s) for s in (1, 2, 3)]
    grad_core = across(out_grad, 1)
    grad_far = across(grad_y, 1)

    kv, kv1, kv2 = call(
        gather_kernel,
        [((2 * BLOCK, DIM), BF16), ((1024, DIM), BF16), ((512, DIM), BF16)],
        name="gather",
    )(meta, *pairs)
    x1 = to_block(kv1, 1, (0, 2))
    x2 = [to_block(kv2, d, range(4 - d)) for d in (1, 2, 3)]

    grads = call(
        grad_kernel,
        [((TOK, DIM), BF16)] * 4,
        [pltpu.VMEM((TOK, 4 * DIM), BF16)],
        name="grad",
        flops=2 * TOK * 512 * 4096,
        bytes_accessed=6 << 20,
    )(meta, out_grad, grad_core, grad_y, grad_far, w_out)
    grad_parts = [grads[0]] + [exchange(grads[s], s) for s in (1, 2, 3)]

    qa, e0, e1, e2, top, out = call(
        own_forward_kernel,
        [
            ((BLOCK, DIM), BF16),
            ((BLOCK, BLOCK), BF16),
            ((512, 512), BF16),
            ((256, 256), BF16),
            ((BLOCK, DIM), F32),
            ((BLOCK, 2 * DIM), F32),
        ],
        [
            pltpu.VMEM((BLOCK, 2 * DIM), BF16),
            pltpu.VMEM((512, 2 * DIM), BF16),
            pltpu.VMEM((256, 2 * DIM), BF16),
        ],
        name="own_forward",
        flops=10**9,
        bytes_accessed=6 << 20,
    )(meta, *query_parts, kv, kv1, kv2)

    doa, dq, factor, delta, g1, g21, g22, g23 = call(
        cross_kernel,
        [
            ((BLOCK, DIM), BF16),
            ((BLOCK, DIM), F32),
            ((BLOCK, DIM), F32),
            ((BLOCK, DIM), F32),
            ((1024, DIM), BF16),
            ((512, DIM), BF16),
            ((512, DIM), BF16),
            ((512, DIM), BF16),
        ],
        [
            pltpu.VMEM((512, DIM), BF16),
            pltpu.VMEM((256, DIM), BF16),
            pltpu.VMEM((512, DIM), BF16),
            pltpu.VMEM((256, DIM), BF16),
            pltpu.VMEM((512, 512), F32),
            pltpu.VMEM((3, 256, 256), F32),
            pltpu.VMEM((512, 512), BF16),
            pltpu.VMEM((3, 256, 256), BF16),
            pltpu.VMEM((BLOCK, DIM), F32),
            pltpu.VMEM((BLOCK, 2 * DIM), F32),
            pltpu.VMEM((BLOCK, DIM), F32),
            pltpu.VMEM((512, 2 * DIM), BF16),
            pltpu.VMEM((3, 256, 2 * DIM), BF16),
        ],
        name="cross",
        flops=10**9,
        bytes_accessed=6 << 20,
    )(meta, qa, x1, *x2, top, out, *grad_parts)
    y1 = to_block(g1, -1, (1, 3))
    y2 = [to_block(g, -d, range(d, 4)) for d, g in ((1, g21), (2, g22), (3, g23))]

    *dq_parts, dkv = call(
        own_backward_kernel,
        [((TOK, DIM), BF16)] * 4 + [((2 * BLOCK, DIM), F32)],
        [
            pltpu.VMEM((BLOCK, DIM), F32),
            pltpu.VMEM((BLOCK, DIM), BF16),
            pltpu.VMEM((BLOCK, DIM), F32),
            pltpu.VMEM((1024, DIM), F32),
            pltpu.VMEM((512, DIM), F32),
            pltpu.VMEM((BLOCK, DIM), BF16),
        ],
        name="own_backward",
        flops=2 * 10**9,
        bytes_accessed=8 << 20,
    )(meta, e0, e1, e2, factor, delta, doa, qa, kv, kv1, kv2, dq)
    dq_parts = [dq_parts[0]] + [exchange(dq_parts[s], s) for s in (1, 2, 3)]

    pairs = call(
        combine_kernel,
        [((2 * TOK, DIM), BF16)] * 4,
        [pltpu.VMEM((2 * BLOCK, DIM), F32)],
        name="combine",
    )(meta, dkv, y1, *y2)
    pairs = [pairs[0]] + [exchange(pairs[s], s) for s in (1, 2, 3)]
    return tuple(
        call(finish_kernel, [((TOK, 4 * DIM), BF16)] * 3, name="finish")(meta, *dq_parts, *pairs)
    )


def solution(mesh):
    return jax.shard_map(
        local,
        mesh=mesh,
        in_specs=(
            P("ctx", "tp"),
            P("ctx", "tp"),
            P("ctx", "tp"),
            P("ctx", "tp"),
            P("tp", None),
            P("tp", None),
        ),
        out_specs=(P("ctx", "tp"), P("ctx", "tp"), P("ctx", "tp")),
        check_vma=False,
    )
```

```python
import math

import jax
import jax.numpy as jnp
from jax import lax
from jax.experimental import pallas as pl
from jax.experimental.pallas import tpu as pltpu
from jax.sharding import PartitionSpec as P

TOK = 256
DIM = 128
BLOCK = 4 * TOK
SCALE = 1.0 / math.sqrt(DIM)
SCALE2 = SCALE * math.log2(math.e)
NEG = -1e30
F32 = jnp.float32
BF16 = jnp.bfloat16


def token_of_row(row):
    return 4 * (row & 63) + 2 * ((row >> 6) & 1) + (row >> 7)


def token_of_row_1(row):
    return 4 * (row & 63) + 2 * (row >> 6)


def iota(shape, dim):
    return lax.broadcasted_iota(jnp.int32, shape, dim)


def dot_nt(a, b):
    return lax.dot_general(a, b, (((1,), (1,)), ((), ())), preferred_element_type=F32)


def dot_nn(a, b):
    return lax.dot_general(a, b, (((1,), (0,)), ((), ())), preferred_element_type=F32)


def dot_tn(a, b):
    return lax.dot_general(a, b, (((0,), (0,)), ((), ())), preferred_element_type=F32)


def rows_at(start, size, unit=64):
    return pl.ds(pl.multiple_of(start, unit), size)


def cols_at(head):
    return pl.ds(pl.multiple_of(head * DIM, DIM), DIM)


def sort_matrix():
    return (iota((TOK, TOK), 1) == token_of_row(iota((TOK, TOK), 0))).astype(BF16)


def unsort_matrix():
    return (iota((TOK, TOK), 0) == token_of_row(iota((TOK, TOK), 1))).astype(BF16)


def wide_max(scores):
    return jnp.broadcast_to(jnp.max(scores, axis=1, keepdims=True), (scores.shape[0], DIM))


def call(kernel, outs, scratch=(), name=None, flops=0, bytes_accessed=0, far=()):
    def run(*args):
        args = [
            pltpu.with_memory_space_constraint(arg, pltpu.HBM) if i in far else arg
            for i, arg in enumerate(args)
        ]
        return pl.pallas_call(
            kernel,
            out_shape=[jax.ShapeDtypeStruct(shape, dtype) for shape, dtype in outs],
            in_specs=[
                pl.BlockSpec(
                    memory_space=pltpu.SMEM
                    if arg.dtype == jnp.int32
                    else pltpu.HBM
                    if i in far
                    else pltpu.VMEM
                )
                for i, arg in enumerate(args)
            ],
            out_specs=[pl.BlockSpec(memory_space=pltpu.VMEM)] * len(outs),
            scratch_shapes=list(scratch),
            compiler_params=pltpu.CompilerParams(vmem_limit_bytes=40 << 20),
            cost_estimate=pl.CostEstimate(
                flops=flops, bytes_accessed=bytes_accessed, transcendentals=0
            ),
            name=name,
        )(*args)

    return run


def seat():
    devices = lax.axis_size("ctx")
    return lax.rem(lax.axis_index("ctx") + (devices - 2), devices)


def place_and_block():
    return seat() & 3, (seat() >> 2) & 3


def head_at(place, block):
    return jnp.where((block & 1) == 1, 3 - place, place)


def places(offsets):
    place, block = place_and_block()
    head = head_at(place, block)
    off2 = offsets[head, 2]
    return place, block, offsets[head, 1], ((off2 & 1) << 1) | (off2 >> 1)


def pack_kernel(q, k, v, o0, o1, o2, o3, held, sem):
    place, block = place_and_block()
    copies = [pltpu.make_async_copy(src, held.at[i], sem.at[i]) for i, src in enumerate((k, v, q))]
    for copy in copies:
        copy.start()
    sort = sort_matrix()
    for i, copy in enumerate(copies):
        copy.wait()
        for s, target in enumerate((o0, o1, o2, o3)):
            head = head_at((place + s) & 3, block)
            rows = held.at[i]
            target[i * TOK : (i + 1) * TOK] = dot_nn(sort, rows[:, cols_at(head)]).astype(BF16)


def gather_kernel(offsets, p0, p1, p2, p3, qa, kv, both, kv2):
    place, _, off1, group2 = places(offsets)
    for s, piece in enumerate((p0, p1, p2, p3)):
        source = (place - s) & 3
        qa[rows_at(source * TOK, TOK)] = piece[2 * TOK :]
        for part in range(2):
            own = piece.at[part * TOK : (part + 1) * TOK]
            kv[rows_at(part * BLOCK + source * TOK, TOK)] = own[...]
            both[rows_at(part * 512 + source * 128, 128)] = own[rows_at(off1 * 128, 128)]
            rows2 = own[rows_at(group2 * 64, 64)]
            both[rows_at(1024 + part * 256 + source * 64, 64)] = rows2
            kv2[rows_at(part * 256 + source * 64, 64)] = rows2


def grad_near_kernel(g0, g1, w, out, w_far, held, sem):
    tp = lax.axis_index("tp")
    width = g0.shape[1]
    slots = (held.at[0], held.at[1], w_far.at[0], w_far.at[1])
    copies = []
    for m, slot in enumerate(slots):
        cols = pl.ds(pl.multiple_of((tp ^ m) * width, width), width)
        copies.append(pltpu.make_async_copy(w.at[:, cols], slot, sem.at[m]))
        copies[m].start()
    copies[0].wait()
    out[...] = dot_nt(g0[...], held[0])
    copies[1].wait()
    out[...] += dot_nt(g1[...], held[1])
    copies[2].wait()
    copies[3].wait()


def grad_far_kernel(near, g2, g3, w, o0, o1, o2, o3, sorted_grad):
    place, block = place_and_block()
    total = near[...] + dot_nt(g2[...], w[0]) + dot_nt(g3[...], w[1])
    sorted_grad[...] = dot_nn(sort_matrix(), total.astype(BF16)).astype(BF16)
    for s, target in enumerate((o0, o1, o2, o3)):
        target[...] = sorted_grad[:, cols_at(head_at((place + s) & 3, block))]


def ones_beside(target, values):
    target[:, :DIM] = values
    target[:, DIM:] = jnp.ones((target.shape[0], DIM), BF16)


def own_forward_kernel(
    offsets, qa, kv, both, e0, e1, e2, top, out, vx0, vx1, vx2
):
    _, _, off1, group2 = places(offsets)
    kv1, kv2 = both.at[:1024], both.at[1024:]
    ones_beside(vx0, kv[BLOCK:])
    ones_beside(vx1, kv1[512:])
    ones_beside(vx2, kv2[256:])
    mask0 = token_of_row(iota((256, 256), 1)) <= token_of_row(iota((256, 256), 0))
    mask1 = token_of_row_1(iota((128, 128), 1)) <= token_of_row_1(iota((128, 128), 0))
    for b in range(4):
        strip = slice(b * 256, (b + 1) * 256)
        rows1 = rows_at(b * 256 + off1 * 128, 128)
        rows2 = rows_at(b * 256 + group2 * 64, 64)
        d1 = slice(b * 128, (b + 1) * 128)
        d2 = slice(b * 64, (b + 1) * 64)
        query, query1, query2 = qa[strip], qa[rows1], qa[rows2]
        near0 = jnp.where(mask0, dot_nt(query, kv[strip]) * SCALE2, NEG)
        near1 = jnp.where(mask1, dot_nt(query1, kv1[d1]) * SCALE2, NEG)
        mask2 = iota((64, 256), 1) <= iota((64, 256), 0) + b * 64
        all2 = jnp.where(mask2, dot_nt(query2, kv2[:256]) * SCALE2, NEG)
        high = wide_max(near0)
        high1 = wide_max(near1)
        if b:
            far0 = dot_nt(query, kv[: b * 256]) * SCALE2
            far1 = dot_nt(query1, kv1[: b * 128]) * SCALE2
            high = jnp.maximum(high, wide_max(far0))
            high1 = jnp.maximum(high1, wide_max(far1))
        top[strip] = high
        top[rows1] = jnp.maximum(top[rows1], high1)
        top[rows2] = jnp.maximum(top[rows2], wide_max(all2))
        top0, top1, top2 = top[strip][:, :1], top[rows1][:, :1], top[rows2][:, :1]
        w = jnp.exp2(near0 - top0).astype(BF16)
        e0[strip, strip] = w
        total = dot_nn(w, vx0[strip])
        if b:
            w = jnp.exp2(far0 - top0).astype(BF16)
            e0[strip, : b * 256] = w
            total = total + dot_nn(w, vx0[: b * 256])
        out[strip] = total
        w = jnp.exp2(near1 - top1).astype(BF16)
        e1[d1, d1] = w
        total = dot_nn(w, vx1[d1])
        if b:
            w = jnp.exp2(far1 - top1).astype(BF16)
            e1[d1, : b * 128] = w
            total = total + dot_nn(w, vx1[: b * 128])
        out[rows1] += total
        w = jnp.exp2(all2 - top2).astype(BF16)
        e2[d2] = w
        out[rows2] += dot_nn(w, vx2[...])


def cross_kernel(
    offsets, qa, xa, xb, xc, top, out, p0, p1, p2, p3,
    doa, dq, factor, delta, ga, gb, gc,
    pq1, pq2, pd1, pd2, sc1, sc2, e1, e2, newtop, newout, inv, vx1, vx2,
):
    place, block, off1, group2 = places(offsets)
    second, later = (block & 1) == 1, block >= 2
    x1, g1 = xa.at[:1024], ga.at[:1024]
    earlier = (
        (second, xa.at[1024:], ga.at[1024:]),
        (later, xb, gb),
        (later, xc, gc),
    )
    for s, piece in enumerate((p0, p1, p2, p3)):
        doa[rows_at(((place - s) & 3) * TOK, TOK)] = piece[...]
    where1 = [rows_at(b * 256 + off1 * 128, 128) for b in range(4)]
    where2 = [rows_at(b * 256 + group2 * 64, 64) for b in range(4)]
    for b in range(4):
        pq1[b * 128 : (b + 1) * 128] = qa[where1[b]]
        pq2[b * 64 : (b + 1) * 64] = qa[where2[b]]
    newtop[...] = top[...]

    @pl.when(second)
    def _():
        ones_beside(vx1, x1[512:])
        sc1[...] = dot_nt(pq1[...], x1[:512]) * SCALE2
        for b in range(4):
            high = wide_max(sc1[b * 128 : (b + 1) * 128])
            newtop[where1[b]] = jnp.maximum(newtop[where1[b]], high)

    for d, (valid, x2, _) in enumerate(earlier):

        @pl.when(valid)
        def _(d=d, x2=x2):
            ones_beside(vx2.at[d], x2[256:])
            sc2[d] = dot_nt(pq2[...], x2[:256]) * SCALE2
            for b in range(4):
                high = wide_max(sc2[d, b * 64 : (b + 1) * 64])
                newtop[where2[b]] = jnp.maximum(newtop[where2[b]], high)

    shrink = jnp.exp2(top[...] - newtop[...])
    newout[:, :DIM] = out[:, :DIM] * shrink
    newout[:, DIM:] = out[:, DIM:] * shrink

    @pl.when(second)
    def _():
        for b in range(4):
            part = slice(b * 128, (b + 1) * 128)
            w = jnp.exp2(sc1[part] - newtop[where1[b]][:, :1]).astype(BF16)
            e1[part] = w
            newout[where1[b]] += dot_nn(w, vx1[...])

    for d, (valid, _, _) in enumerate(earlier):

        @pl.when(valid)
        def _(d=d):
            for b in range(4):
                part = slice(b * 64, (b + 1) * 64)
                w = jnp.exp2(sc2[d, part] - newtop[where2[b]][:, :1]).astype(BF16)
                e2[d, part] = w
                newout[where2[b]] += dot_nn(w, vx2[d])

    inv[...] = 1.0 / newout[:, DIM:]
    grads = doa[...].astype(F32)
    row_delta = jnp.sum(grads * newout[:, :DIM] * inv[...], axis=1, keepdims=True)
    delta[...] = jnp.broadcast_to(row_delta, delta.shape)
    factor[...] = shrink * inv[...]
    dq[...] = jnp.zeros(dq.shape, F32)
    for b in range(4):
        pd1[b * 128 : (b + 1) * 128] = (doa[where1[b]].astype(F32) * inv[where1[b]]).astype(BF16)
        pd2[b * 64 : (b + 1) * 64] = (doa[where2[b]].astype(F32) * inv[where2[b]]).astype(BF16)

    @pl.when(second)
    def _():
        prob = dot_nt(pd1[...], x1[512:])
        level = jnp.concatenate([(delta[r] * inv[r])[:, :1] for r in where1], axis=0)
        score_grad = (e1[...].astype(F32) * (prob - level)).astype(BF16)
        part = dot_nn(score_grad, x1[:512])
        for b in range(4):
            dq[where1[b]] += part[b * 128 : (b + 1) * 128]
        g1[:512] = (dot_tn(score_grad, pq1[...]) * SCALE).astype(BF16)
        g1[512:] = dot_tn(e1[...], pd1[...]).astype(BF16)

    for d, (valid, x2, g2) in enumerate(earlier):

        @pl.when(valid)
        def _(d=d, x2=x2, g2=g2):
            prob = dot_nt(pd2[...], x2[256:])
            level = jnp.concatenate([(delta[r] * inv[r])[:, :1] for r in where2], axis=0)
            score_grad = (e2[d].astype(F32) * (prob - level)).astype(BF16)
            part = dot_nn(score_grad, x2[:256])
            for b in range(4):
                dq[where2[b]] += part[b * 64 : (b + 1) * 64]
            g2[:256] = (dot_tn(score_grad, pq2[...]) * SCALE).astype(BF16)
            g2[256:] = dot_tn(e2[d], pd2[...]).astype(BF16)


def own_backward_kernel(
    offsets, e0, e1, e2, factor, delta, doa, qa, kv, both, dq_in,
    o0, o1, o2, o3, dkv, dq, low, shift, dkv1, dkv2, low_q,
):
    place, _, off1, group2 = places(offsets)
    kv1, kv2 = both.at[:1024], both.at[1024:]
    low[...] = (doa[...].astype(F32) * factor[...]).astype(BF16)
    shift[...] = factor[...] * delta[...]
    dq[...] = dq_in[...]
    for b in range(3, -1, -1):
        strip = slice(b * 256, (b + 1) * 256)
        n0, n1 = (b + 1) * 256, (b + 1) * 128
        rows1 = rows_at(b * 256 + off1 * 128, 128)
        rows2 = rows_at(b * 256 + group2 * 64, 64)
        d1 = slice(b * 128, (b + 1) * 128)
        d2 = slice(b * 64, (b + 1) * 64)
        parts = (
            (strip, strip, e0, kv, BLOCK, n0, dkv),
            (rows1, d1, e1, kv1, 512, n1, dkv1),
            (rows2, d2, e2, kv2, 256, 256, dkv2),
        )
        for rows, part, weights, pair, half, count, grads in parts:
            grad_low = low[rows]
            prob = dot_nt(grad_low, pair[half : half + count])
            w = weights[part, :count]
            score_grad = (w.astype(F32) * (prob - shift[rows][:, :1])).astype(BF16)
            dq[rows] += dot_nn(score_grad, pair[:count])
            key_term = dot_tn(score_grad, qa[rows])
            value_term = dot_tn(w, grad_low)
            if b == 3:
                grads[:count] = key_term
                grads[half : half + count] = value_term
            else:
                grads[:count] += key_term
                grads[half : half + count] += value_term
    for p in range(4):
        for part in range(2):
            dkv[rows_at(part * BLOCK + p * 256 + off1 * 128, 128)] += dkv1[
                part * 512 + p * 128 : part * 512 + (p + 1) * 128
            ]
            dkv[rows_at(part * BLOCK + p * 256 + group2 * 64, 64)] += dkv2[
                part * 256 + p * 64 : part * 256 + (p + 1) * 64
            ]
    dkv[:BLOCK] = dkv[:BLOCK] * SCALE
    low_q[...] = (dq[...] * SCALE).astype(BF16)
    for s, target in enumerate((o0, o1, o2, o3)):
        target[...] = low_q[rows_at(((place + s) & 3) * TOK, TOK)]


def combine_kernel(offsets, dkv, last_q, ya, yb, yc, o0, o1, o2, o3, total):
    home, _, off1, group2 = places(offsets)
    y1, y2 = ya.at[:1024], ya.at[1024:]
    total[...] = dkv[...]
    for p in range(4):
        for part in range(2):
            one = slice(part * 512 + p * 128, part * 512 + (p + 1) * 128)
            two = slice(part * 256 + p * 64, part * 256 + (p + 1) * 64)
            total[rows_at(part * BLOCK + p * 256 + off1 * 128, 128)] += y1[one].astype(F32)
            total[rows_at(part * BLOCK + p * 256 + group2 * 64, 64)] += (
                y2[two].astype(F32) + yb[two].astype(F32) + yc[two].astype(F32)
            )
    for s, target in enumerate((o0, o1, o2, o3)):
        place = (home + s) & 3
        for part in range(2):
            target[part * TOK : (part + 1) * TOK] = total[
                rows_at(part * BLOCK + place * TOK, TOK)
            ].astype(BF16)
    o3[2 * TOK :] = last_q[...]


def unsort_pieces(pieces, outs):
    place, block = place_and_block()
    unsort = unsort_matrix()
    for s, piece in enumerate(pieces):
        cols = cols_at(head_at((place - s) & 3, block))
        for i, out in enumerate(outs):
            out[:, cols] = dot_nn(unsort, piece[i * TOK : (i + 1) * TOK]).astype(BF16)


def finish_query_kernel(p0, p1, p2, dq):
    unsort_pieces((p0, p1, p2), (dq,))


def finish_kernel(dq_in, p0, p1, p2, p3, dq, dk, dv):
    dq[...] = dq_in[...]
    unsort_pieces((p0, p1, p2, p3), (dk, dv))
    place, block = place_and_block()
    last = dot_nn(unsort_matrix(), p3[2 * TOK :]).astype(BF16)
    dq[:, cols_at(head_at((place - 3) & 3, block))] = last


def local(queries, keys, values, out_grad, w_out, offsets):
    devices = lax.axis_size("ctx")

    def at(index):
        return (index + 2) % devices

    def exchange(part, s):
        route = [(at(u), at(u // 4 * 4 + (u % 4 + s) % 4)) for u in range(devices)]
        return lax.ppermute(part, "ctx", route)

    def to_blocks(part, pairs, back=False):
        route = []
        for first in range(0, devices, 16):
            for source, target in pairs:
                for place in range(4):
                    there = 3 - place if (source + target) % 2 else place
                    pair = (at(first + 4 * source + place), at(first + 4 * target + there))
                    route.append(pair[::-1] if back else pair)
        return lax.ppermute(part, "ctx", route)

    def across(part, m):
        return lax.ppermute(part, "tp", [(i, i ^ m) for i in range(4)])

    def after(part, *others):
        return lax.optimization_barrier((part, *others))[0]

    links = (((0, 1), (2, 3)), ((1, 2), (0, 3)), ((0, 2), (1, 3)))
    width = out_grad.shape[1]
    half = (2, 4 * DIM, width)

    grad_y = across(out_grad, 2)
    packed = call(
        pack_kernel,
        [((3 * TOK, DIM), BF16)] * 4,
        [pltpu.VMEM((3, TOK, 4 * DIM), BF16), pltpu.SemaphoreType.DMA((3,))],
        name="pack",
        flops=2 * 10**8,
        bytes_accessed=2 << 20,
        far=(0, 1, 2),
    )(queries, keys, values)
    pieces = [exchange(packed[s], s) for s in (1, 2, 3)]
    grad_core = across(after(out_grad, packed[1]), 1)
    near, w_far = call(
        grad_near_kernel,
        [((TOK, 4 * DIM), F32), (half, BF16)],
        [pltpu.VMEM(half, BF16), pltpu.SemaphoreType.DMA((4,))],
        name="grad_near",
        far=(2,),
    )(out_grad, grad_core, w_out)
    grad_far = across(after(grad_y, near, *pieces), 1)
    grads = call(
        grad_far_kernel,
        [((TOK, DIM), BF16)] * 4,
        [pltpu.VMEM((TOK, 4 * DIM), BF16)],
        name="grad_far",
        flops=TOK * 512 * 4096,
        bytes_accessed=4 << 20,
    )(near, grad_y, grad_far, w_far)

    qa, kv, both, kv2 = call(
        gather_kernel,
        [
            ((BLOCK, DIM), BF16),
            ((2 * BLOCK, DIM), BF16),
            ((1536, DIM), BF16),
            ((512, DIM), BF16),
        ],
        name="gather",
        flops=10**7,
        bytes_accessed=2 << 20,
    )(offsets, packed[0], after(pieces[0], near), *pieces[1:])
    xs = [to_blocks(part, pairs) for part, pairs in zip((both, kv2, kv2), links)]
    grad_parts = [grads[0]] + [exchange(after(grads[s], kv2), s) for s in (1, 2, 3)]

    e0, e1, e2, top, out = call(
        own_forward_kernel,
        [
            ((BLOCK, BLOCK), BF16),
            ((512, 512), BF16),
            ((256, 256), BF16),
            ((BLOCK, DIM), F32),
            ((BLOCK, 2 * DIM), F32),
        ],
        [
            pltpu.VMEM((BLOCK, 2 * DIM), BF16),
            pltpu.VMEM((512, 2 * DIM), BF16),
            pltpu.VMEM((256, 2 * DIM), BF16),
        ],
        name="own_forward",
        flops=10**9,
        bytes_accessed=6 << 20,
    )(offsets, qa, kv, both)

    doa, dq, factor, delta, *partials = call(
        cross_kernel,
        [
            ((BLOCK, DIM), BF16),
            ((BLOCK, DIM), F32),
            ((BLOCK, DIM), F32),
            ((BLOCK, DIM), F32),
            ((1536, DIM), BF16),
            ((512, DIM), BF16),
            ((512, DIM), BF16),
        ],
        [
            pltpu.VMEM((512, DIM), BF16),
            pltpu.VMEM((256, DIM), BF16),
            pltpu.VMEM((512, DIM), BF16),
            pltpu.VMEM((256, DIM), BF16),
            pltpu.VMEM((512, 512), F32),
            pltpu.VMEM((3, 256, 256), F32),
            pltpu.VMEM((512, 512), BF16),
            pltpu.VMEM((3, 256, 256), BF16),
            pltpu.VMEM((BLOCK, DIM), F32),
            pltpu.VMEM((BLOCK, 2 * DIM), F32),
            pltpu.VMEM((BLOCK, DIM), F32),
            pltpu.VMEM((512, 2 * DIM), BF16),
            pltpu.VMEM((3, 256, 2 * DIM), BF16),
        ],
        name="cross",
        flops=10**9,
        bytes_accessed=6 << 20,
    )(offsets, qa, *xs, top, out, *grad_parts)
    ys = [to_blocks(part, pairs, back=True) for part, pairs in zip(partials, links)]

    *dq_parts, dkv = call(
        own_backward_kernel,
        [((TOK, DIM), BF16)] * 4 + [((2 * BLOCK, DIM), F32)],
        [
            pltpu.VMEM((BLOCK, DIM), F32),
            pltpu.VMEM((BLOCK, DIM), BF16),
            pltpu.VMEM((BLOCK, DIM), F32),
            pltpu.VMEM((1024, DIM), F32),
            pltpu.VMEM((512, DIM), F32),
            pltpu.VMEM((BLOCK, DIM), BF16),
        ],
        name="own_backward",
        flops=2 * 10**9,
        bytes_accessed=8 << 20,
    )(offsets, e0, e1, e2, factor, delta, doa, qa, kv, both, dq)
    near_parts = [dq_parts[0]] + [exchange(dq_parts[s], s) for s in (1, 2)]

    pairs = call(
        combine_kernel,
        [((2 * TOK, DIM), BF16)] * 3 + [((3 * TOK, DIM), BF16)],
        [pltpu.VMEM((2 * BLOCK, DIM), F32)],
        name="combine",
        flops=10**7,
        bytes_accessed=4 << 20,
    )(offsets, after(dkv, *near_parts), dq_parts[3], *ys)
    query_grad = call(finish_query_kernel, [((TOK, 4 * DIM), BF16)], name="finish_query")(
        near_parts[0], after(near_parts[1], pairs[0]), near_parts[2]
    )[0]
    pairs = [pairs[0]] + [exchange(pairs[s], s) for s in (1, 2, 3)]
    pairs[1] = after(pairs[1], query_grad)
    return tuple(
        call(finish_kernel, [((TOK, 4 * DIM), BF16)] * 3, name="finish")(query_grad, *pairs)
    )


def solution(mesh):
    return jax.shard_map(
        local,
        mesh=mesh,
        in_specs=(
            P("ctx", "tp"),
            P("ctx", "tp"),
            P("ctx", "tp"),
            P("ctx", "tp"),
            P("tp", None),
            P("tp", None),
        ),
        out_specs=(P("ctx", "tp"), P("ctx", "tp"), P("ctx", "tp")),
        check_vma=False,
    )
```

```python
import math

import jax
import jax.numpy as jnp
from jax import lax
from jax.experimental import pallas as pl
from jax.experimental.pallas import tpu as pltpu
from jax.sharding import PartitionSpec as P

TOK = 256
DIM = 128
BLOCK = 4 * TOK
SCALE = 1.0 / math.sqrt(DIM)
SCALE2 = SCALE * math.log2(math.e)
NEG = -1e30
F32 = jnp.float32
BF16 = jnp.bfloat16


def token_of_row(row):
    return 4 * (row & 63) + 2 * ((row >> 6) & 1) + (row >> 7)


def token_of_row_1(row):
    return 4 * (row & 63) + 2 * (row >> 6)


def iota(shape, dim):
    return lax.broadcasted_iota(jnp.int32, shape, dim)


def dot_nt(a, b):
    return lax.dot_general(a, b, (((1,), (1,)), ((), ())), preferred_element_type=F32)


def dot_nn(a, b):
    return lax.dot_general(a, b, (((1,), (0,)), ((), ())), preferred_element_type=F32)


def dot_tn(a, b):
    return lax.dot_general(a, b, (((0,), (0,)), ((), ())), preferred_element_type=F32)


def rows_at(start, size, unit=64):
    return pl.ds(pl.multiple_of(start, unit), size)


def cols_at(head):
    return pl.ds(pl.multiple_of(head * DIM, DIM), DIM)


def sort_matrix():
    return (iota((TOK, TOK), 1) == token_of_row(iota((TOK, TOK), 0))).astype(BF16)


def unsort_matrix():
    return (iota((TOK, TOK), 0) == token_of_row(iota((TOK, TOK), 1))).astype(BF16)


def wide_max(scores):
    return jnp.broadcast_to(jnp.max(scores, axis=1, keepdims=True), (scores.shape[0], DIM))


def call(kernel, outs, scratch=(), name=None, flops=0, bytes_accessed=0, far=()):
    def run(*args):
        args = [
            pltpu.with_memory_space_constraint(arg, pltpu.HBM) if i in far else arg
            for i, arg in enumerate(args)
        ]
        return pl.pallas_call(
            kernel,
            out_shape=[jax.ShapeDtypeStruct(shape, dtype) for shape, dtype in outs],
            in_specs=[
                pl.BlockSpec(
                    memory_space=pltpu.SMEM
                    if arg.dtype == jnp.int32
                    else pltpu.HBM
                    if i in far
                    else pltpu.VMEM
                )
                for i, arg in enumerate(args)
            ],
            out_specs=[pl.BlockSpec(memory_space=pltpu.VMEM)] * len(outs),
            scratch_shapes=list(scratch),
            compiler_params=pltpu.CompilerParams(vmem_limit_bytes=16 << 20),
            cost_estimate=pl.CostEstimate(
                flops=flops, bytes_accessed=bytes_accessed, transcendentals=0
            ),
            name=name,
        )(*args)

    return run


def seat():
    devices = lax.axis_size("ctx")
    return lax.rem(lax.axis_index("ctx") + (devices - 2), devices)


def place_and_block():
    return seat() & 3, (seat() >> 2) & 3


def head_at(place, block):
    return jnp.where((block & 1) == 1, 3 - place, place)


def places(offsets):
    place, block = place_and_block()
    head = head_at(place, block)
    off2 = offsets[head, 2]
    return place, block, offsets[head, 1], ((off2 & 1) << 1) | (off2 >> 1)


def pack_kernel(q, k, v, o0, o1, o2, o3, held, sem):
    place, block = place_and_block()
    copies = [pltpu.make_async_copy(src, held.at[i], sem.at[i]) for i, src in enumerate((k, v, q))]
    for copy in copies:
        copy.start()
    sort = sort_matrix()
    for i, copy in enumerate(copies):
        copy.wait()
        for s, target in enumerate((o0, o1, o2, o3)):
            head = head_at((place + s) & 3, block)
            rows = held.at[i]
            target[i * TOK : (i + 1) * TOK] = dot_nn(sort, rows[:, cols_at(head)]).astype(BF16)


def gather_kernel(offsets, p0, p1, p2, p3, qa, kv, both, kv2):
    place, _, off1, group2 = places(offsets)
    for s, piece in enumerate((p0, p1, p2, p3)):
        source = (place - s) & 3
        qa[rows_at(source * TOK, TOK)] = piece[2 * TOK :]
        for part in range(2):
            own = piece.at[part * TOK : (part + 1) * TOK]
            kv[rows_at(part * BLOCK + source * TOK, TOK)] = own[...]
            both[rows_at(part * 512 + source * 128, 128)] = own[rows_at(off1 * 128, 128)]
            rows2 = own[rows_at(group2 * 64, 64)]
            both[rows_at(1024 + part * 256 + source * 64, 64)] = rows2
            kv2[rows_at(part * 256 + source * 64, 64)] = rows2


def grad_near_kernel(g0, g1, w, out, w_far, held, sem):
    tp = lax.axis_index("tp")
    width = g0.shape[1]
    slots = (held.at[0], held.at[1], w_far.at[0], w_far.at[1])
    copies = []
    for m, slot in enumerate(slots):
        cols = pl.ds(pl.multiple_of((tp ^ m) * width, width), width)
        copies.append(pltpu.make_async_copy(w.at[:, cols], slot, sem.at[m]))
        copies[m].start()
    copies[0].wait()
    out[...] = dot_nt(g0[...], held[0])
    copies[1].wait()
    out[...] += dot_nt(g1[...], held[1])
    copies[2].wait()
    copies[3].wait()


def grad_far_kernel(near, g2, g3, w, o0, o1, o2, o3, sorted_grad):
    place, block = place_and_block()
    total = near[...] + dot_nt(g2[...], w[0]) + dot_nt(g3[...], w[1])
    sorted_grad[...] = dot_nn(sort_matrix(), total.astype(BF16)).astype(BF16)
    for s, target in enumerate((o0, o1, o2, o3)):
        target[...] = sorted_grad[:, cols_at(head_at((place + s) & 3, block))]


def ones_beside(target, values):
    target[:, :DIM] = values
    target[:, DIM:] = jnp.ones((target.shape[0], DIM), BF16)


def own_forward_kernel(
    offsets, qa, kv, both, e0, e1, e2, top, out, vx0, vx1, vx2
):
    _, _, off1, group2 = places(offsets)
    kv1, kv2 = both.at[:1024], both.at[1024:]
    ones_beside(vx0, kv[BLOCK:])
    ones_beside(vx1, kv1[512:])
    ones_beside(vx2, kv2[256:])
    mask0 = token_of_row(iota((256, 256), 1)) <= token_of_row(iota((256, 256), 0))
    mask1 = token_of_row_1(iota((128, 128), 1)) <= token_of_row_1(iota((128, 128), 0))
    for b in range(4):
        strip = slice(b * 256, (b + 1) * 256)
        rows1 = rows_at(b * 256 + off1 * 128, 128)
        rows2 = rows_at(b * 256 + group2 * 64, 64)
        d1 = slice(b * 128, (b + 1) * 128)
        d2 = slice(b * 64, (b + 1) * 64)
        query, query1, query2 = qa[strip], qa[rows1], qa[rows2]
        near0 = jnp.where(mask0, dot_nt(query, kv[strip]) * SCALE2, NEG)
        near1 = jnp.where(mask1, dot_nt(query1, kv1[d1]) * SCALE2, NEG)
        mask2 = iota((64, 256), 1) <= iota((64, 256), 0) + b * 64
        all2 = jnp.where(mask2, dot_nt(query2, kv2[:256]) * SCALE2, NEG)
        high = wide_max(near0)
        high1 = wide_max(near1)
        if b:
            far0 = dot_nt(query, kv[: b * 256]) * SCALE2
            far1 = dot_nt(query1, kv1[: b * 128]) * SCALE2
            high = jnp.maximum(high, wide_max(far0))
            high1 = jnp.maximum(high1, wide_max(far1))
        top[strip] = high
        top[rows1] = jnp.maximum(top[rows1], high1)
        top[rows2] = jnp.maximum(top[rows2], wide_max(all2))
        top0, top1, top2 = top[strip][:, :1], top[rows1][:, :1], top[rows2][:, :1]
        w = jnp.exp2(near0 - top0).astype(BF16)
        e0[strip, strip] = w
        total = dot_nn(w, vx0[strip])
        if b:
            w = jnp.exp2(far0 - top0).astype(BF16)
            e0[strip, : b * 256] = w
            total = total + dot_nn(w, vx0[: b * 256])
        out[strip] = total
        w = jnp.exp2(near1 - top1).astype(BF16)
        e1[d1, d1] = w
        total = dot_nn(w, vx1[d1])
        if b:
            w = jnp.exp2(far1 - top1).astype(BF16)
            e1[d1, : b * 128] = w
            total = total + dot_nn(w, vx1[: b * 128])
        out[rows1] += total
        w = jnp.exp2(all2 - top2).astype(BF16)
        e2[d2] = w
        out[rows2] += dot_nn(w, vx2[...])


def cross_kernel(
    offsets, qa, xa, xb, xc, top, out, p0, p1, p2, p3,
    doa, dq, factor, delta, ga, gb, gc,
    pq1, pq2, pd1, pd2, sc1, sc2, e1, e2, newtop, newout, inv, vx1, vx2,
):
    place, block, off1, group2 = places(offsets)
    where1 = [rows_at(b * 256 + off1 * 128, 128) for b in range(4)]
    where2 = [rows_at(b * 256 + group2 * 64, 64) for b in range(4)]
    one = (xa.at[:1024], ga.at[:1024], sc1, e1, vx1, where1, pq1, pd1)
    two = [
        (x, g, sc2.at[d], e2.at[d], vx2.at[d], where2, pq2, pd2)
        for d, (x, g) in enumerate(((xa.at[1024:], ga.at[1024:]), (xb, gb), (xc, gc)))
    ]
    groups = (((block & 1) == 1, (one, two[0])), (block >= 2, two[1:]))
    for s, piece in enumerate((p0, p1, p2, p3)):
        doa[rows_at(((place - s) & 3) * TOK, TOK)] = piece[...]
    for b in range(4):
        pq1[b * 128 : (b + 1) * 128] = qa[where1[b]]
        pq2[b * 64 : (b + 1) * 64] = qa[where2[b]]
    newtop[...] = top[...]

    for valid, tiles in groups:

        @pl.when(valid)
        def _(tiles=tiles):
            highs = []
            for x, _, scores, _, values, _, queries, _ in tiles:
                half = x.shape[0] // 2
                ones_beside(values, x[half:])
                product = dot_nt(queries[...], x[:half]) * SCALE2
                scores[...] = product
                highs.append(wide_max(product))
            for high, (_, _, _, _, _, where, _, _) in zip(highs, tiles):
                size = high.shape[0] // 4
                for b in range(4):
                    part = high[b * size : (b + 1) * size]
                    newtop[where[b]] = jnp.maximum(newtop[where[b]], part)

    shrink = jnp.exp2(top[...] - newtop[...])
    newout[:, :DIM] = out[:, :DIM] * shrink
    newout[:, DIM:] = out[:, DIM:] * shrink

    for valid, tiles in groups:

        @pl.when(valid)
        def _(tiles=tiles):
            sums = []
            for _, _, scores, weights, values, where, _, _ in tiles:
                level = jnp.concatenate([newtop[r][:, :1] for r in where], axis=0)
                w = jnp.exp2(scores[...] - level).astype(BF16)
                weights[...] = w
                sums.append(dot_nn(w, values[...]))
            for total, (_, _, _, _, _, where, _, _) in zip(sums, tiles):
                size = total.shape[0] // 4
                for b in range(4):
                    newout[where[b]] += total[b * size : (b + 1) * size]

    inv[...] = 1.0 / newout[:, DIM:]
    grads = doa[...].astype(F32)
    row_delta = jnp.sum(grads * newout[:, :DIM] * inv[...], axis=1, keepdims=True)
    delta[...] = jnp.broadcast_to(row_delta, delta.shape)
    factor[...] = shrink * inv[...]
    dq[...] = jnp.zeros(dq.shape, F32)
    for b in range(4):
        pd1[b * 128 : (b + 1) * 128] = (doa[where1[b]].astype(F32) * inv[where1[b]]).astype(BF16)
        pd2[b * 64 : (b + 1) * 64] = (doa[where2[b]].astype(F32) * inv[where2[b]]).astype(BF16)

    for valid, tiles in groups:

        @pl.when(valid)
        def _(tiles=tiles):
            parts = []
            for x, g, _, weights, _, where, queries, grad_low in tiles:
                half = x.shape[0] // 2
                prob = dot_nt(grad_low[...], x[half:])
                level = jnp.concatenate([(delta[r] * inv[r])[:, :1] for r in where], axis=0)
                w = weights[...]
                score_grad = (w.astype(F32) * (prob - level)).astype(BF16)
                g[half:] = dot_tn(w, grad_low[...]).astype(BF16)
                g[:half] = (dot_tn(score_grad, queries[...]) * SCALE).astype(BF16)
                parts.append(dot_nn(score_grad, x[:half]))
            for part, (_, _, _, _, _, where, _, _) in zip(parts, tiles):
                size = part.shape[0] // 4
                for b in range(4):
                    dq[where[b]] += part[b * size : (b + 1) * size]


def own_backward_kernel(
    offsets, e0, e1, e2, factor, delta, doa, qa, kv, both, dq_in,
    o0, o1, o2, o3, dkv, dq, low, shift, dkv1, dkv2,
):
    place, _, off1, group2 = places(offsets)
    kv1, kv2 = both.at[:1024], both.at[1024:]
    low[...] = (doa[...].astype(F32) * factor[...]).astype(BF16)
    shift[...] = factor[...] * delta[...]
    dq[...] = dq_in[...]
    for b in range(3, -1, -1):
        strip = slice(b * 256, (b + 1) * 256)
        n0, n1 = (b + 1) * 256, (b + 1) * 128
        rows1 = rows_at(b * 256 + off1 * 128, 128)
        rows2 = rows_at(b * 256 + group2 * 64, 64)
        d1 = slice(b * 128, (b + 1) * 128)
        d2 = slice(b * 64, (b + 1) * 64)
        parts = (
            (strip, strip, e0, kv, BLOCK, n0, dkv),
            (rows1, d1, e1, kv1, 512, n1, dkv1),
            (rows2, d2, e2, kv2, 256, 256, dkv2),
        )
        for rows, part, weights, pair, half, count, grads in parts:
            grad_low = low[rows]
            prob = dot_nt(grad_low, pair[half : half + count])
            w = weights[part, :count]
            score_grad = (w.astype(F32) * (prob - shift[rows][:, :1])).astype(BF16)
            dq[rows] += dot_nn(score_grad, pair[:count])
            key_term = dot_tn(score_grad, qa[rows])
            value_term = dot_tn(w, grad_low)
            if b == 3:
                grads[:count] = key_term
                grads[half : half + count] = value_term
            else:
                grads[:count] += key_term
                grads[half : half + count] += value_term
    for p in range(4):
        for part in range(2):
            dkv[rows_at(part * BLOCK + p * 256 + off1 * 128, 128)] += dkv1[
                part * 512 + p * 128 : part * 512 + (p + 1) * 128
            ]
            dkv[rows_at(part * BLOCK + p * 256 + group2 * 64, 64)] += dkv2[
                part * 256 + p * 64 : part * 256 + (p + 1) * 64
            ]
    for s, target in enumerate((o0, o1, o2, o3)):
        at = ((place + s) & 3) * TOK
        target[:TOK] = (dkv[rows_at(at, TOK)] * SCALE).astype(BF16)
        target[TOK : 2 * TOK] = dkv[rows_at(BLOCK + at, TOK)].astype(BF16)
        target[2 * TOK :] = (dq[rows_at(at, TOK)] * SCALE).astype(BF16)


def combine_kernel(ya, yb, yc, o0, o1, o2, o3):
    place, _ = place_and_block()
    for s, target in enumerate((o0, o1, o2, o3)):
        token = (place + s) & 3
        for part in range(2):
            one = rows_at(part * 512 + token * 128, 128)
            two = part * 256 + token * 64
            target[part * 128 : (part + 1) * 128] = ya[one]
            target[256 + part * 64 : 256 + (part + 1) * 64] = (
                ya[rows_at(1024 + two, 64)].astype(F32)
                + yb[rows_at(two, 64)].astype(F32)
                + yc[rows_at(two, 64)].astype(F32)
            ).astype(BF16)


def finish_query_kernel(p0, p1, p2, p3, dq):
    place, block = place_and_block()
    unsort = unsort_matrix()
    for s, piece in enumerate((p0, p1, p2, p3)):
        cols = cols_at(head_at((place - s) & 3, block))
        dq[:, cols] = dot_nn(unsort, piece[2 * TOK :]).astype(BF16)


def finish_kernel(offsets, p0, p1, p2, p3, c0, c1, c2, c3, dk, dv, total):
    place, block = place_and_block()
    unsort = unsort_matrix()
    for s, (piece, cross) in enumerate(((p0, c0), (p1, c1), (p2, c2), (p3, c3))):
        head = head_at((place - s) & 3, block)
        off1, off2 = offsets[head, 1], offsets[head, 2]
        group2 = ((off2 & 1) << 1) | (off2 >> 1)
        cols = cols_at(head)
        for part, out in enumerate((dk, dv)):
            both = total.at[2 * s + part]
            both[...] = piece[part * TOK : (part + 1) * TOK].astype(F32)
            rows1, rows2 = rows_at(off1 * 128, 128), rows_at(group2 * 64, 64)
            both[rows1] += cross[part * 128 : (part + 1) * 128].astype(F32)
            both[rows2] += cross[256 + part * 64 : 256 + (part + 1) * 64].astype(F32)
            out[:, cols] = dot_nn(unsort, both[...].astype(BF16)).astype(BF16)


def local(queries, keys, values, out_grad, w_out, offsets):
    devices = lax.axis_size("ctx")

    def at(index):
        return (index + 2) % devices

    def exchange(part, s, blocks=(0, 1, 2, 3)):
        route = [
            (at(u), at(u // 4 * 4 + (u % 4 + s) % 4))
            for u in range(devices)
            if u // 4 % 4 in blocks
        ]
        return lax.ppermute(part, "ctx", route)

    def to_blocks(part, pairs, back=False):
        route = []
        for first in range(0, devices, 16):
            for source, target in pairs:
                for place in range(4):
                    there = 3 - place if (source + target) % 2 else place
                    pair = (at(first + 4 * source + place), at(first + 4 * target + there))
                    route.append(pair[::-1] if back else pair)
        return lax.ppermute(part, "ctx", route)

    def across(part, m):
        return lax.ppermute(part, "tp", [(i, i ^ m) for i in range(4)])

    def after(part, *others):
        return lax.optimization_barrier((part, *others))[0]

    links = (((0, 1), (2, 3)), ((1, 2), (0, 3)), ((0, 2), (1, 3)))
    width = out_grad.shape[1]
    half = (2, 4 * DIM, width)

    grad_y = across(out_grad, 2)
    packed = call(
        pack_kernel,
        [((3 * TOK, DIM), BF16)] * 4,
        [pltpu.VMEM((3, TOK, 4 * DIM), BF16), pltpu.SemaphoreType.DMA((3,))],
        name="pack",
        flops=2 * 10**8,
        bytes_accessed=2 << 20,
        far=(0, 1, 2),
    )(queries, keys, values)
    pieces = [exchange(packed[s], s) for s in (1, 2, 3)]
    grad_core = across(after(out_grad, packed[1]), 1)
    near, w_far = call(
        grad_near_kernel,
        [((TOK, 4 * DIM), F32), (half, BF16)],
        [pltpu.VMEM(half, BF16), pltpu.SemaphoreType.DMA((4,))],
        name="grad_near",
        far=(2,),
    )(out_grad, grad_core, w_out)
    grad_far = across(after(grad_y, near, *pieces), 1)
    grads = call(
        grad_far_kernel,
        [((TOK, DIM), BF16)] * 4,
        [pltpu.VMEM((TOK, 4 * DIM), BF16)],
        name="grad_far",
        flops=TOK * 512 * 4096,
        bytes_accessed=4 << 20,
    )(near, grad_y, grad_far, w_far)

    qa, kv, both, kv2 = call(
        gather_kernel,
        [
            ((BLOCK, DIM), BF16),
            ((2 * BLOCK, DIM), BF16),
            ((1536, DIM), BF16),
            ((512, DIM), BF16),
        ],
        name="gather",
        flops=10**7,
        bytes_accessed=2 << 20,
    )(offsets, packed[0], after(pieces[0], near), *pieces[1:])
    first, rest = after(both, grads[1]), after(kv2, grads[1])
    xs = [to_blocks(part, pairs) for part, pairs in zip((first, rest, rest), links)]
    grad_parts = [grads[0]] + [exchange(grads[s], s) for s in (1, 2, 3)]

    e0, e1, e2, top, out = call(
        own_forward_kernel,
        [
            ((BLOCK, BLOCK), BF16),
            ((512, 512), BF16),
            ((256, 256), BF16),
            ((BLOCK, DIM), F32),
            ((BLOCK, 2 * DIM), F32),
        ],
        [
            pltpu.VMEM((BLOCK, 2 * DIM), BF16),
            pltpu.VMEM((512, 2 * DIM), BF16),
            pltpu.VMEM((256, 2 * DIM), BF16),
        ],
        name="own_forward",
        flops=10**9,
        bytes_accessed=6 << 20,
    )(offsets, qa, kv, both)

    doa, dq, factor, delta, *partials = call(
        cross_kernel,
        [
            ((BLOCK, DIM), BF16),
            ((BLOCK, DIM), F32),
            ((BLOCK, DIM), F32),
            ((BLOCK, DIM), F32),
            ((1536, DIM), BF16),
            ((512, DIM), BF16),
            ((512, DIM), BF16),
        ],
        [
            pltpu.VMEM((512, DIM), BF16),
            pltpu.VMEM((256, DIM), BF16),
            pltpu.VMEM((512, DIM), BF16),
            pltpu.VMEM((256, DIM), BF16),
            pltpu.VMEM((512, 512), F32),
            pltpu.VMEM((3, 256, 256), F32),
            pltpu.VMEM((512, 512), BF16),
            pltpu.VMEM((3, 256, 256), BF16),
            pltpu.VMEM((BLOCK, DIM), F32),
            pltpu.VMEM((BLOCK, 2 * DIM), F32),
            pltpu.VMEM((BLOCK, DIM), F32),
            pltpu.VMEM((512, 2 * DIM), BF16),
            pltpu.VMEM((3, 256, 2 * DIM), BF16),
        ],
        name="cross",
        flops=10**9,
        bytes_accessed=6 << 20,
    )(offsets, qa, *xs, top, out, *grad_parts)
    ys = [to_blocks(part, pairs, back=True) for part, pairs in zip(partials, links)]

    own_parts = call(
        own_backward_kernel,
        [((3 * TOK, DIM), BF16)] * 4,
        [
            pltpu.VMEM((2 * BLOCK, DIM), F32),
            pltpu.VMEM((BLOCK, DIM), F32),
            pltpu.VMEM((BLOCK, DIM), BF16),
            pltpu.VMEM((BLOCK, DIM), F32),
            pltpu.VMEM((1024, DIM), F32),
            pltpu.VMEM((512, DIM), F32),
        ],
        name="own_backward",
        flops=2 * 10**9,
        bytes_accessed=8 << 20,
    )(offsets, e0, e1, e2, factor, delta, doa, qa, kv, both, dq)
    own_parts = list(own_parts)
    own_parts[3] = after(own_parts[3], *ys[1:])
    own_parts = [own_parts[0]] + [exchange(own_parts[s], s) for s in (1, 2, 3)]

    cross_parts = call(
        combine_kernel,
        [((384, DIM), BF16)] * 4,
        name="combine",
        flops=10**7,
        bytes_accessed=1 << 20,
    )(after(ys[0], *own_parts[:3]), *ys[1:])
    cross_parts = [cross_parts[0]] + [
        exchange(cross_parts[s], s, (0, 1, 2)) for s in (1, 2, 3)
    ]
    query_grad = call(finish_query_kernel, [((TOK, 4 * DIM), BF16)], name="finish_query")(
        *own_parts
    )[0]
    cross_parts[1] = after(cross_parts[1], query_grad)
    key_value_grads = call(
        finish_kernel,
        [((TOK, 4 * DIM), BF16)] * 2,
        [pltpu.VMEM((8, TOK, DIM), F32)],
        name="finish",
    )(offsets, *own_parts, *cross_parts)
    return (query_grad, *key_value_grads)


def solution(mesh):
    return jax.shard_map(
        local,
        mesh=mesh,
        in_specs=(
            P("ctx", "tp"),
            P("ctx", "tp"),
            P("ctx", "tp"),
            P("ctx", "tp"),
            P("tp", None),
            P("tp", None),
        ),
        out_specs=(P("ctx", "tp"), P("ctx", "tp"), P("ctx", "tp")),
        check_vma=False,
    )
```

```python
import math

import jax
import jax.numpy as jnp
from jax import lax
from jax.experimental import pallas as pl
from jax.experimental.pallas import tpu as pltpu
from jax.sharding import PartitionSpec as P

TOK = 256
DIM = 128
BLOCK = 4 * TOK
SCALE = 1.0 / math.sqrt(DIM)
SCALE2 = SCALE * math.log2(math.e)
NEG = -1e30
F32 = jnp.float32
BF16 = jnp.bfloat16


def token_of_row(row):
    return 4 * (row & 63) + 2 * ((row >> 6) & 1) + (row >> 7)


def token_of_row_1(row):
    return 4 * (row & 63) + 2 * (row >> 6)


def iota(shape, dim):
    return lax.broadcasted_iota(jnp.int32, shape, dim)


def dot_nt(a, b):
    return lax.dot_general(a, b, (((1,), (1,)), ((), ())), preferred_element_type=F32)


def dot_nn(a, b):
    return lax.dot_general(a, b, (((1,), (0,)), ((), ())), preferred_element_type=F32)


def dot_tn(a, b):
    return lax.dot_general(a, b, (((0,), (0,)), ((), ())), preferred_element_type=F32)


def rows_at(start, size, unit=64):
    return pl.ds(pl.multiple_of(start, unit), size)


def cols_at(head):
    return pl.ds(pl.multiple_of(head * DIM, DIM), DIM)


def sort_matrix():
    return (iota((TOK, TOK), 1) == token_of_row(iota((TOK, TOK), 0))).astype(BF16)


def unsort_matrix():
    return (iota((TOK, TOK), 0) == token_of_row(iota((TOK, TOK), 1))).astype(BF16)


def wide_max(scores):
    return jnp.broadcast_to(jnp.max(scores, axis=1, keepdims=True), (scores.shape[0], DIM))


def call(
    kernel, outs, scratch=(), name=None, flops=0, bytes_accessed=0, far=(), outs_far=False
):
    def run(*args):
        args = [
            pltpu.with_memory_space_constraint(arg, pltpu.HBM) if i in far else arg
            for i, arg in enumerate(args)
        ]
        return pl.pallas_call(
            kernel,
            out_shape=[jax.ShapeDtypeStruct(shape, dtype) for shape, dtype in outs],
            in_specs=[
                pl.BlockSpec(
                    memory_space=pltpu.SMEM
                    if arg.dtype == jnp.int32
                    else pltpu.HBM
                    if i in far
                    else pltpu.VMEM
                )
                for i, arg in enumerate(args)
            ],
            out_specs=[pl.BlockSpec(memory_space=pltpu.HBM if outs_far else pltpu.VMEM)]
            * len(outs),
            scratch_shapes=list(scratch),
            compiler_params=pltpu.CompilerParams(vmem_limit_bytes=16 << 20),
            cost_estimate=pl.CostEstimate(
                flops=flops, bytes_accessed=bytes_accessed, transcendentals=0
            ),
            name=name,
        )(*args)

    return run


def seat():
    devices = lax.axis_size("ctx")
    return lax.rem(lax.axis_index("ctx") + (devices - 2), devices)


def place_and_block():
    return seat() & 3, (seat() >> 2) & 3


def head_at(place, block):
    return jnp.where((block & 1) == 1, 3 - place, place)


def places(offsets):
    place, block = place_and_block()
    head = head_at(place, block)
    off2 = offsets[head, 2]
    return place, block, offsets[head, 1], ((off2 & 1) << 1) | (off2 >> 1)


def pack_kernel(q, k, v, o0, o1, o2, o3, held, sem):
    place, block = place_and_block()
    copies = [pltpu.make_async_copy(src, held.at[i], sem.at[i]) for i, src in enumerate((k, v, q))]
    for copy in copies:
        copy.start()
    sort = sort_matrix()
    for i, copy in enumerate(copies):
        copy.wait()
        held[i] = dot_nn(sort, held[i]).astype(BF16)
        for s, target in enumerate((o0, o1, o2, o3)):
            rows = held.at[i]
            target[i * TOK : (i + 1) * TOK] = rows[:, cols_at(head_at((place + s) & 3, block))]


def gather_kernel(offsets, p0, p1, p2, p3, qa, kv, both, kv2):
    place, _, off1, group2 = places(offsets)
    for s, piece in enumerate((p0, p1, p2, p3)):
        source = (place - s) & 3
        qa[rows_at(source * TOK, TOK)] = piece[2 * TOK :]
        for part in range(2):
            own = piece.at[part * TOK : (part + 1) * TOK]
            kv[rows_at(part * BLOCK + source * TOK, TOK)] = own[...]
            both[rows_at(part * 512 + source * 128, 128)] = own[rows_at(off1 * 128, 128)]
            rows2 = own[rows_at(group2 * 64, 64)]
            both[rows_at(1024 + part * 256 + source * 64, 64)] = rows2
            kv2[rows_at(part * 256 + source * 64, 64)] = rows2


def grad_near_kernel(g0, g1, w, out, w_far, held, sem):
    tp = lax.axis_index("tp")
    width = g0.shape[1]
    slots = (held.at[0], held.at[1], w_far.at[0], w_far.at[1])
    copies = []
    for m, slot in enumerate(slots):
        cols = pl.ds(pl.multiple_of((tp ^ m) * width, width), width)
        copies.append(pltpu.make_async_copy(w.at[:, cols], slot, sem.at[m]))
        copies[m].start()
    copies[0].wait()
    out[...] = dot_nt(g0[...], held[0])
    copies[1].wait()
    out[...] += dot_nt(g1[...], held[1])
    copies[2].wait()
    copies[3].wait()


def grad_far_kernel(near, g2, g3, w, o0, o1, o2, o3, sorted_grad):
    place, block = place_and_block()
    total = near[...] + dot_nt(g2[...], w[0]) + dot_nt(g3[...], w[1])
    sorted_grad[...] = dot_nn(sort_matrix(), total.astype(BF16)).astype(BF16)
    for s, target in enumerate((o0, o1, o2, o3)):
        target[...] = sorted_grad[:, cols_at(head_at((place + s) & 3, block))]


def ones_beside(target, values):
    target[:, :DIM] = values
    target[:, DIM:] = jnp.ones((target.shape[0], DIM), BF16)


def own_forward_kernel(
    offsets, qa, kv, both, e0, e1, e2, top, out, vx0, vx1, vx2
):
    _, _, off1, group2 = places(offsets)
    kv1, kv2 = both.at[:1024], both.at[1024:]
    ones_beside(vx0, kv[BLOCK:])
    ones_beside(vx1, kv1[512:])
    ones_beside(vx2, kv2[256:])
    mask0 = token_of_row(iota((256, 256), 1)) <= token_of_row(iota((256, 256), 0))
    mask1 = token_of_row_1(iota((128, 128), 1)) <= token_of_row_1(iota((128, 128), 0))
    for b in range(4):
        strip = slice(b * 256, (b + 1) * 256)
        rows1 = rows_at(b * 256 + off1 * 128, 128)
        rows2 = rows_at(b * 256 + group2 * 64, 64)
        d1 = slice(b * 128, (b + 1) * 128)
        d2 = slice(b * 64, (b + 1) * 64)
        query, query1, query2 = qa[strip], qa[rows1], qa[rows2]
        near0 = jnp.where(mask0, dot_nt(query, kv[strip]) * SCALE2, NEG)
        near1 = jnp.where(mask1, dot_nt(query1, kv1[d1]) * SCALE2, NEG)
        mask2 = iota((64, 256), 1) <= iota((64, 256), 0) + b * 64
        all2 = jnp.where(mask2, dot_nt(query2, kv2[:256]) * SCALE2, NEG)
        high = wide_max(near0)
        high1 = wide_max(near1)
        if b:
            far0 = dot_nt(query, kv[: b * 256]) * SCALE2
            far1 = dot_nt(query1, kv1[: b * 128]) * SCALE2
            high = jnp.maximum(high, wide_max(far0))
            high1 = jnp.maximum(high1, wide_max(far1))
        top[strip] = high
        top[rows1] = jnp.maximum(top[rows1], high1)
        top[rows2] = jnp.maximum(top[rows2], wide_max(all2))
        top0, top1, top2 = top[strip][:, :1], top[rows1][:, :1], top[rows2][:, :1]
        w = jnp.exp2(near0 - top0).astype(BF16)
        e0[strip, strip] = w
        total = dot_nn(w, vx0[strip])
        if b:
            w = jnp.exp2(far0 - top0).astype(BF16)
            e0[strip, : b * 256] = w
            total = total + dot_nn(w, vx0[: b * 256])
        out[strip] = total
        w = jnp.exp2(near1 - top1).astype(BF16)
        e1[d1, d1] = w
        total = dot_nn(w, vx1[d1])
        if b:
            w = jnp.exp2(far1 - top1).astype(BF16)
            e1[d1, : b * 128] = w
            total = total + dot_nn(w, vx1[: b * 128])
        out[rows1] += total
        w = jnp.exp2(all2 - top2).astype(BF16)
        e2[d2] = w
        out[rows2] += dot_nn(w, vx2[...])


def cross_kernel(
    offsets, qa, xa, xb, xc, top, out, p0, p1, p2, p3,
    doa, dq, factor, delta, ga, gb, gc,
    pq1, pq2, pd1, pd2, sc1, sc2, e1, e2, newtop, newout, inv, vx1, vx2,
):
    place, block, off1, group2 = places(offsets)
    where1 = [rows_at(b * 256 + off1 * 128, 128) for b in range(4)]
    where2 = [rows_at(b * 256 + group2 * 64, 64) for b in range(4)]
    one = (xa.at[:1024], ga.at[:1024], sc1, e1, vx1, where1, pq1, pd1)
    two = [
        (x, g, sc2.at[d], e2.at[d], vx2.at[d], where2, pq2, pd2)
        for d, (x, g) in enumerate(((xa.at[1024:], ga.at[1024:]), (xb, gb), (xc, gc)))
    ]
    groups = (((block & 1) == 1, (one, two[0])), (block >= 2, two[1:]))
    for s, piece in enumerate((p0, p1, p2, p3)):
        doa[rows_at(((place - s) & 3) * TOK, TOK)] = piece[...]
    for b in range(4):
        pq1[b * 128 : (b + 1) * 128] = qa[where1[b]]
        pq2[b * 64 : (b + 1) * 64] = qa[where2[b]]
    newtop[...] = top[...]

    for valid, tiles in groups:

        @pl.when(valid)
        def _(tiles=tiles):
            highs = []
            for x, _, scores, _, values, _, queries, _ in tiles:
                half = x.shape[0] // 2
                ones_beside(values, x[half:])
                product = dot_nt(queries[...], x[:half]) * SCALE2
                scores[...] = product
                highs.append(wide_max(product))
            for high, (_, _, _, _, _, where, _, _) in zip(highs, tiles):
                size = high.shape[0] // 4
                for b in range(4):
                    part = high[b * size : (b + 1) * size]
                    newtop[where[b]] = jnp.maximum(newtop[where[b]], part)

    shrink = jnp.exp2(top[...] - newtop[...])
    newout[:, :DIM] = out[:, :DIM] * shrink
    newout[:, DIM:] = out[:, DIM:] * shrink

    for valid, tiles in groups:

        @pl.when(valid)
        def _(tiles=tiles):
            sums = []
            for _, _, scores, weights, values, where, _, _ in tiles:
                level = jnp.concatenate([newtop[r][:, :1] for r in where], axis=0)
                w = jnp.exp2(scores[...] - level).astype(BF16)
                weights[...] = w
                sums.append(dot_nn(w, values[...]))
            for total, (_, _, _, _, _, where, _, _) in zip(sums, tiles):
                size = total.shape[0] // 4
                for b in range(4):
                    newout[where[b]] += total[b * size : (b + 1) * size]

    inv[...] = 1.0 / newout[:, DIM:]
    grads = doa[...].astype(F32)
    row_delta = jnp.sum(grads * newout[:, :DIM] * inv[...], axis=1, keepdims=True)
    delta[...] = jnp.broadcast_to(row_delta, delta.shape)
    factor[...] = shrink * inv[...]
    dq[...] = jnp.zeros(dq.shape, F32)
    for b in range(4):
        pd1[b * 128 : (b + 1) * 128] = (doa[where1[b]].astype(F32) * inv[where1[b]]).astype(BF16)
        pd2[b * 64 : (b + 1) * 64] = (doa[where2[b]].astype(F32) * inv[where2[b]]).astype(BF16)

    for valid, tiles in groups:

        @pl.when(valid)
        def _(tiles=tiles):
            parts = []
            for x, g, _, weights, _, where, queries, grad_low in tiles:
                half = x.shape[0] // 2
                prob = dot_nt(grad_low[...], x[half:])
                level = jnp.concatenate([(delta[r] * inv[r])[:, :1] for r in where], axis=0)
                w = weights[...]
                score_grad = (w.astype(F32) * (prob - level)).astype(BF16)
                g[half:] = dot_tn(w, grad_low[...]).astype(BF16)
                g[:half] = (dot_tn(score_grad, queries[...]) * SCALE).astype(BF16)
                parts.append(dot_nn(score_grad, x[:half]))
            for part, (_, _, _, _, _, where, _, _) in zip(parts, tiles):
                size = part.shape[0] // 4
                for b in range(4):
                    dq[where[b]] += part[b * size : (b + 1) * size]


def own_backward_kernel(
    offsets, e0, e1, e2, factor, delta, doa, qa, kv, both, dq_in,
    o0, o1, o2, o3, dkv, dq, low, shift, dkv1, dkv2,
):
    place, _, off1, group2 = places(offsets)
    kv1, kv2 = both.at[:1024], both.at[1024:]
    low[...] = (doa[...].astype(F32) * factor[...]).astype(BF16)
    shift[...] = factor[...] * delta[...]
    dq[...] = dq_in[...]
    for b in range(3, -1, -1):
        strip = slice(b * 256, (b + 1) * 256)
        n0, n1 = (b + 1) * 256, (b + 1) * 128
        rows1 = rows_at(b * 256 + off1 * 128, 128)
        rows2 = rows_at(b * 256 + group2 * 64, 64)
        d1 = slice(b * 128, (b + 1) * 128)
        d2 = slice(b * 64, (b + 1) * 64)
        parts = (
            (strip, strip, e0, kv, BLOCK, n0, dkv),
            (rows1, d1, e1, kv1, 512, n1, dkv1),
            (rows2, d2, e2, kv2, 256, 256, dkv2),
        )
        for rows, part, weights, pair, half, count, grads in parts:
            grad_low = low[rows]
            prob = dot_nt(grad_low, pair[half : half + count])
            w = weights[part, :count]
            score_grad = (w.astype(F32) * (prob - shift[rows][:, :1])).astype(BF16)
            dq[rows] += dot_nn(score_grad, pair[:count])
            key_term = dot_tn(score_grad, qa[rows])
            value_term = dot_tn(w, grad_low)
            if b == 3:
                grads[:count] = key_term
                grads[half : half + count] = value_term
            else:
                grads[:count] += key_term
                grads[half : half + count] += value_term
    for p in range(4):
        for part in range(2):
            dkv[rows_at(part * BLOCK + p * 256 + off1 * 128, 128)] += dkv1[
                part * 512 + p * 128 : part * 512 + (p + 1) * 128
            ]
            dkv[rows_at(part * BLOCK + p * 256 + group2 * 64, 64)] += dkv2[
                part * 256 + p * 64 : part * 256 + (p + 1) * 64
            ]
    for s, target in enumerate((o0, o1, o2, o3)):
        at = ((place + s) & 3) * TOK
        target[:TOK] = (dkv[rows_at(at, TOK)] * SCALE).astype(BF16)
        target[TOK : 2 * TOK] = dkv[rows_at(BLOCK + at, TOK)].astype(BF16)
        target[2 * TOK :] = (dq[rows_at(at, TOK)] * SCALE).astype(BF16)


def combine_kernel(ya, yb, yc, o0, o1, o2, o3):
    place, _ = place_and_block()
    for s, target in enumerate((o0, o1, o2, o3)):
        token = (place + s) & 3
        for part in range(2):
            one = rows_at(part * 512 + token * 128, 128)
            two = part * 256 + token * 64
            target[part * 128 : (part + 1) * 128] = ya[one]
            target[256 + part * 64 : 256 + (part + 1) * 64] = (
                ya[rows_at(1024 + two, 64)].astype(F32)
                + yb[rows_at(two, 64)].astype(F32)
                + yc[rows_at(two, 64)].astype(F32)
            ).astype(BF16)


def finish_own_kernel(p0, p1, p2, p3, dq, dk, dv, held):
    place, block = place_and_block()
    for s, piece in enumerate((p0, p1, p2, p3)):
        cols = cols_at(head_at((place - s) & 3, block))
        dk[:, cols] = piece[:TOK].astype(F32)
        dv[:, cols] = piece[TOK : 2 * TOK].astype(F32)
        held[:, cols] = piece[2 * TOK :]
    dq[...] = dot_nn(unsort_matrix(), held[...]).astype(BF16)


def finish_kernel(offsets, in_k, in_v, c0, c1, c2, c3, dk, dv, total, low_k, low_v, sem):
    place, block = place_and_block()
    unsort = unsort_matrix()
    copies = []
    for part, (own, low, out) in enumerate(((in_k, low_k, dk), (in_v, low_v, dv))):
        total[part] = own[...]
        for s, cross in enumerate((c0, c1, c2, c3)):
            head = head_at((place - s) & 3, block)
            off1, off2 = offsets[head, 1], offsets[head, 2]
            group2 = ((off2 & 1) << 1) | (off2 >> 1)
            cols = cols_at(head)
            rows1, rows2 = rows_at(off1 * 128, 128), rows_at(group2 * 64, 64)
            sums = total.at[part]
            sums[rows1, cols] += cross[part * 128 : (part + 1) * 128].astype(F32)
            sums[rows2, cols] += cross[256 + part * 64 : 256 + (part + 1) * 64].astype(F32)
        low[...] = dot_nn(unsort, total[part].astype(BF16)).astype(BF16)
        copies.append(pltpu.make_async_copy(low, out, sem.at[part]))
        copies[part].start()
    for copy in copies:
        copy.wait()


def local(queries, keys, values, out_grad, w_out, offsets):
    devices = lax.axis_size("ctx")

    def at(index):
        return (index + 2) % devices

    def exchange(part, s, blocks=(0, 1, 2, 3)):
        route = [
            (at(u), at(u // 4 * 4 + (u % 4 + s) % 4))
            for u in range(devices)
            if u // 4 % 4 in blocks
        ]
        return lax.ppermute(part, "ctx", route)

    def to_blocks(part, pairs, back=False):
        route = []
        for first in range(0, devices, 16):
            for source, target in pairs:
                for place in range(4):
                    there = 3 - place if (source + target) % 2 else place
                    pair = (at(first + 4 * source + place), at(first + 4 * target + there))
                    route.append(pair[::-1] if back else pair)
        return lax.ppermute(part, "ctx", route)

    def across(part, m):
        return lax.ppermute(part, "tp", [(i, i ^ m) for i in range(4)])

    def after(part, *others):
        return lax.optimization_barrier((part, *others))[0]

    links = (((0, 1), (2, 3)), ((1, 2), (0, 3)), ((0, 2), (1, 3)))
    width = out_grad.shape[1]
    half = (2, 4 * DIM, width)

    grad_y = across(out_grad, 2)
    packed = call(
        pack_kernel,
        [((3 * TOK, DIM), BF16)] * 4,
        [pltpu.VMEM((3, TOK, 4 * DIM), BF16), pltpu.SemaphoreType.DMA((3,))],
        name="pack",
        flops=2 * 10**8,
        bytes_accessed=2 << 20,
        far=(0, 1, 2),
    )(queries, keys, values)
    pieces = [exchange(packed[s], s) for s in (1, 2, 3)]
    grad_core = across(after(out_grad, packed[1]), 1)
    near, w_far = call(
        grad_near_kernel,
        [((TOK, 4 * DIM), F32), (half, BF16)],
        [pltpu.VMEM(half, BF16), pltpu.SemaphoreType.DMA((4,))],
        name="grad_near",
        far=(2,),
    )(out_grad, grad_core, w_out)
    grad_far = across(after(grad_y, near, *pieces), 1)
    grads = call(
        grad_far_kernel,
        [((TOK, DIM), BF16)] * 4,
        [pltpu.VMEM((TOK, 4 * DIM), BF16)],
        name="grad_far",
        flops=TOK * 512 * 4096,
        bytes_accessed=4 << 20,
    )(near, grad_y, grad_far, w_far)

    qa, kv, both, kv2 = call(
        gather_kernel,
        [
            ((BLOCK, DIM), BF16),
            ((2 * BLOCK, DIM), BF16),
            ((1536, DIM), BF16),
            ((512, DIM), BF16),
        ],
        name="gather",
        flops=10**7,
        bytes_accessed=2 << 20,
    )(offsets, packed[0], after(pieces[0], near), *pieces[1:])
    first, rest = after(both, grads[1]), after(kv2, grads[1])
    xs = [to_blocks(part, pairs) for part, pairs in zip((first, rest, rest), links)]
    grad_parts = [grads[0]] + [exchange(grads[s], s) for s in (1, 2, 3)]

    e0, e1, e2, top, out = call(
        own_forward_kernel,
        [
            ((BLOCK, BLOCK), BF16),
            ((512, 512), BF16),
            ((256, 256), BF16),
            ((BLOCK, DIM), F32),
            ((BLOCK, 2 * DIM), F32),
        ],
        [
            pltpu.VMEM((BLOCK, 2 * DIM), BF16),
            pltpu.VMEM((512, 2 * DIM), BF16),
            pltpu.VMEM((256, 2 * DIM), BF16),
        ],
        name="own_forward",
        flops=10**9,
        bytes_accessed=6 << 20,
    )(offsets, qa, kv, both)

    doa, dq, factor, delta, *partials = call(
        cross_kernel,
        [
            ((BLOCK, DIM), BF16),
            ((BLOCK, DIM), F32),
            ((BLOCK, DIM), F32),
            ((BLOCK, DIM), F32),
            ((1536, DIM), BF16),
            ((512, DIM), BF16),
            ((512, DIM), BF16),
        ],
        [
            pltpu.VMEM((512, DIM), BF16),
            pltpu.VMEM((256, DIM), BF16),
            pltpu.VMEM((512, DIM), BF16),
            pltpu.VMEM((256, DIM), BF16),
            pltpu.VMEM((512, 512), F32),
            pltpu.VMEM((3, 256, 256), F32),
            pltpu.VMEM((512, 512), BF16),
            pltpu.VMEM((3, 256, 256), BF16),
            pltpu.VMEM((BLOCK, DIM), F32),
            pltpu.VMEM((BLOCK, 2 * DIM), F32),
            pltpu.VMEM((BLOCK, DIM), F32),
            pltpu.VMEM((512, 2 * DIM), BF16),
            pltpu.VMEM((3, 256, 2 * DIM), BF16),
        ],
        name="cross",
        flops=10**9,
        bytes_accessed=6 << 20,
    )(offsets, qa, *xs, top, out, *grad_parts)
    ys = [to_blocks(part, pairs, back=True) for part, pairs in zip(partials, links)]

    own_parts = call(
        own_backward_kernel,
        [((3 * TOK, DIM), BF16)] * 4,
        [
            pltpu.VMEM((2 * BLOCK, DIM), F32),
            pltpu.VMEM((BLOCK, DIM), F32),
            pltpu.VMEM((BLOCK, DIM), BF16),
            pltpu.VMEM((BLOCK, DIM), F32),
            pltpu.VMEM((1024, DIM), F32),
            pltpu.VMEM((512, DIM), F32),
        ],
        name="own_backward",
        flops=2 * 10**9,
        bytes_accessed=8 << 20,
    )(offsets, e0, e1, e2, factor, delta, doa, qa, kv, both, dq)
    own_parts = list(own_parts)
    own_parts[3] = after(own_parts[3], *ys[1:])
    own_parts = [own_parts[0]] + [exchange(own_parts[s], s) for s in (1, 2, 3)]

    cross_parts = call(
        combine_kernel,
        [((384, DIM), BF16)] * 4,
        name="combine",
        flops=10**7,
        bytes_accessed=1 << 20,
    )(after(ys[0], *own_parts[:3]), *ys[1:])
    cross_parts = [cross_parts[0]] + [
        exchange(cross_parts[s], s, (0, 1, 2)) for s in (1, 2, 3)
    ]
    wide = (TOK, 4 * DIM)
    query_grad, own_k, own_v = call(
        finish_own_kernel,
        [(wide, BF16), (wide, F32), (wide, F32)],
        [pltpu.VMEM(wide, BF16)],
        name="finish_own",
    )(*own_parts)
    cross_parts[1] = after(cross_parts[1], query_grad)
    key_value_grads = call(
        finish_kernel,
        [(wide, BF16)] * 2,
        [
            pltpu.VMEM((2, *wide), F32),
            pltpu.VMEM(wide, BF16),
            pltpu.VMEM(wide, BF16),
            pltpu.SemaphoreType.DMA((2,)),
        ],
        name="finish",
        outs_far=True,
    )(
        offsets, own_k, own_v, *cross_parts
    )
    return (query_grad, *key_value_grads)


def solution(mesh):
    return jax.shard_map(
        local,
        mesh=mesh,
        in_specs=(
            P("ctx", "tp"),
            P("ctx", "tp"),
            P("ctx", "tp"),
            P("ctx", "tp"),
            P("tp", None),
            P("tp", None),
        ),
        out_specs=(P("ctx", "tp"), P("ctx", "tp"), P("ctx", "tp")),
        check_vma=False,
    )
```

```python
import math

import jax
import jax.numpy as jnp
from jax import lax
from jax.experimental import pallas as pl
from jax.experimental.pallas import tpu as pltpu
from jax.sharding import PartitionSpec as P

TOK = 256
DIM = 128
BLOCK = 4 * TOK
SCALE = 1.0 / math.sqrt(DIM)
SCALE2 = SCALE * math.log2(math.e)
NEG = -1e30
F32 = jnp.float32
BF16 = jnp.bfloat16


def token_of_row(row):
    return 4 * (row & 63) + 2 * ((row >> 6) & 1) + (row >> 7)


def token_of_row_1(row):
    return 4 * (row & 63) + 2 * (row >> 6)


def iota(shape, dim):
    return lax.broadcasted_iota(jnp.int32, shape, dim)


def dot_nt(a, b):
    return lax.dot_general(a, b, (((1,), (1,)), ((), ())), preferred_element_type=F32)


def dot_nn(a, b):
    return lax.dot_general(a, b, (((1,), (0,)), ((), ())), preferred_element_type=F32)


def dot_tn(a, b):
    return lax.dot_general(a, b, (((0,), (0,)), ((), ())), preferred_element_type=F32)


def rows_at(start, size, unit=64):
    return pl.ds(pl.multiple_of(start, unit), size)


def cols_at(head):
    return pl.ds(pl.multiple_of(head * DIM, DIM), DIM)


def sort_matrix():
    return (iota((TOK, TOK), 1) == token_of_row(iota((TOK, TOK), 0))).astype(BF16)


def unsort_matrix():
    return (iota((TOK, TOK), 0) == token_of_row(iota((TOK, TOK), 1))).astype(BF16)


def wide_max(scores):
    return jnp.broadcast_to(jnp.max(scores, axis=1, keepdims=True), (scores.shape[0], DIM))


def call(
    kernel, outs, scratch=(), name=None, flops=0, bytes_accessed=0, far=(), outs_far=False
):
    def run(*args):
        args = [
            pltpu.with_memory_space_constraint(arg, pltpu.HBM) if i in far else arg
            for i, arg in enumerate(args)
        ]
        return pl.pallas_call(
            kernel,
            out_shape=[jax.ShapeDtypeStruct(shape, dtype) for shape, dtype in outs],
            in_specs=[
                pl.BlockSpec(
                    memory_space=pltpu.SMEM
                    if arg.dtype == jnp.int32
                    else pltpu.HBM
                    if i in far
                    else pltpu.VMEM
                )
                for i, arg in enumerate(args)
            ],
            out_specs=[pl.BlockSpec(memory_space=pltpu.HBM if outs_far else pltpu.VMEM)]
            * len(outs),
            scratch_shapes=list(scratch),
            compiler_params=pltpu.CompilerParams(vmem_limit_bytes=16 << 20),
            cost_estimate=pl.CostEstimate(
                flops=flops, bytes_accessed=bytes_accessed, transcendentals=0
            ),
            name=name,
        )(*args)

    return run


def seat():
    devices = lax.axis_size("ctx")
    return lax.rem(lax.axis_index("ctx") + (devices - 2), devices)


def place_and_block():
    return seat() & 3, (seat() >> 2) & 3


def head_at(place, block):
    return jnp.where((block & 1) == 1, 3 - place, place)


def places(offsets):
    place, block = place_and_block()
    head = head_at(place, block)
    off2 = offsets[head, 2]
    return place, block, offsets[head, 1], ((off2 & 1) << 1) | (off2 >> 1)


def pack_kernel(q, k, v, o0, o1, o2, o3, held, sem):
    place, block = place_and_block()
    copies = [pltpu.make_async_copy(src, held.at[i], sem.at[i]) for i, src in enumerate((k, v, q))]
    for copy in copies:
        copy.start()
    sort = sort_matrix()
    for i, copy in enumerate(copies):
        copy.wait()
        held[i] = dot_nn(sort, held[i]).astype(BF16)
        for s, target in enumerate((o0, o1, o2, o3)):
            rows = held.at[i]
            target[i * TOK : (i + 1) * TOK] = rows[:, cols_at(head_at((place + s) & 3, block))]


def gather_kernel(offsets, p0, p1, p2, p3, qa, kv, both, kv2):
    place, _, off1, group2 = places(offsets)
    for s, piece in enumerate((p0, p1, p2, p3)):
        source = (place - s) & 3
        qa[rows_at(source * TOK, TOK)] = piece[2 * TOK :]
        for part in range(2):
            own = piece.at[part * TOK : (part + 1) * TOK]
            kv[rows_at(part * BLOCK + source * TOK, TOK)] = own[...]
            both[rows_at(part * 512 + source * 128, 128)] = own[rows_at(off1 * 128, 128)]
            rows2 = own[rows_at(group2 * 64, 64)]
            both[rows_at(1024 + part * 256 + source * 64, 64)] = rows2
            kv2[rows_at(part * 256 + source * 64, 64)] = rows2


def grad_near_kernel(g0, g1, w, out, w_far, held, sem):
    tp = lax.axis_index("tp")
    width = g0.shape[1]
    slots = (held.at[0], held.at[1], w_far.at[0], w_far.at[1])
    copies = []
    for m, slot in enumerate(slots):
        cols = pl.ds(pl.multiple_of((tp ^ m) * width, width), width)
        copies.append(pltpu.make_async_copy(w.at[:, cols], slot, sem.at[m]))
        copies[m].start()
    copies[0].wait()
    out[...] = dot_nt(g0[...], held[0])
    copies[1].wait()
    out[...] += dot_nt(g1[...], held[1])
    copies[2].wait()
    copies[3].wait()


def grad_far_kernel(near, g2, g3, w, o0, o1, o2, o3, sorted_grad):
    place, block = place_and_block()
    total = near[...] + dot_nt(g2[...], w[0]) + dot_nt(g3[...], w[1])
    sorted_grad[...] = dot_nn(sort_matrix(), total.astype(BF16)).astype(BF16)
    for s, target in enumerate((o0, o1, o2, o3)):
        target[...] = sorted_grad[:, cols_at(head_at((place + s) & 3, block))]


def ones_beside(target, values):
    target[:, :DIM] = values
    target[:, DIM:] = jnp.ones((target.shape[0], DIM), BF16)


def own_forward_kernel(
    offsets, qa, kv, both, e0, e1, e2, top, out, vx0, vx1, vx2
):
    _, _, off1, group2 = places(offsets)
    kv1, kv2 = both.at[:1024], both.at[1024:]
    ones_beside(vx0, kv[BLOCK:])
    ones_beside(vx1, kv1[512:])
    ones_beside(vx2, kv2[256:])
    mask0 = token_of_row(iota((256, 256), 1)) <= token_of_row(iota((256, 256), 0))
    mask1 = token_of_row_1(iota((128, 128), 1)) <= token_of_row_1(iota((128, 128), 0))
    for b in range(4):
        strip = slice(b * 256, (b + 1) * 256)
        rows1 = rows_at(b * 256 + off1 * 128, 128)
        rows2 = rows_at(b * 256 + group2 * 64, 64)
        d1 = slice(b * 128, (b + 1) * 128)
        d2 = slice(b * 64, (b + 1) * 64)
        query, query1, query2 = qa[strip], qa[rows1], qa[rows2]
        near0 = jnp.where(mask0, dot_nt(query, kv[strip]) * SCALE2, NEG)
        near1 = jnp.where(mask1, dot_nt(query1, kv1[d1]) * SCALE2, NEG)
        mask2 = iota((64, 256), 1) <= iota((64, 256), 0) + b * 64
        all2 = jnp.where(mask2, dot_nt(query2, kv2[:256]) * SCALE2, NEG)
        high = wide_max(near0)
        high1 = wide_max(near1)
        if b:
            far0 = dot_nt(query, kv[: b * 256]) * SCALE2
            far1 = dot_nt(query1, kv1[: b * 128]) * SCALE2
            high = jnp.maximum(high, wide_max(far0))
            high1 = jnp.maximum(high1, wide_max(far1))
        top[strip] = high
        top[rows1] = jnp.maximum(top[rows1], high1)
        top[rows2] = jnp.maximum(top[rows2], wide_max(all2))
        top0, top1, top2 = top[strip][:, :1], top[rows1][:, :1], top[rows2][:, :1]
        w = jnp.exp2(near0 - top0).astype(BF16)
        e0[strip, strip] = w
        total = dot_nn(w, vx0[strip])
        if b:
            w = jnp.exp2(far0 - top0).astype(BF16)
            e0[strip, : b * 256] = w
            total = total + dot_nn(w, vx0[: b * 256])
        out[strip] = total
        w = jnp.exp2(near1 - top1).astype(BF16)
        e1[d1, d1] = w
        total = dot_nn(w, vx1[d1])
        if b:
            w = jnp.exp2(far1 - top1).astype(BF16)
            e1[d1, : b * 128] = w
            total = total + dot_nn(w, vx1[: b * 128])
        out[rows1] += total
        w = jnp.exp2(all2 - top2).astype(BF16)
        e2[d2] = w
        out[rows2] += dot_nn(w, vx2[...])


def cross_kernel(
    offsets, qa, xa, xb, xc, top, out, p0, p1, p2, p3,
    doa, dq, factor, delta, ga, gb, gc,
    pq1, pq2, pd1, pd2, sc1, sc2, e1, e2, newtop, newout, inv, vx1, vx2,
):
    place, block, off1, group2 = places(offsets)
    where1 = [rows_at(b * 256 + off1 * 128, 128) for b in range(4)]
    where2 = [rows_at(b * 256 + group2 * 64, 64) for b in range(4)]
    one = (xa.at[:1024], ga.at[:1024], sc1, e1, vx1, where1, pq1, pd1)
    two = [
        (x, g, sc2.at[d], e2.at[d], vx2.at[d], where2, pq2, pd2)
        for d, (x, g) in enumerate(((xa.at[1024:], ga.at[1024:]), (xb, gb), (xc, gc)))
    ]
    groups = (((block & 1) == 1, (one, two[0])), (block >= 2, two[1:]))
    for s, piece in enumerate((p0, p1, p2, p3)):
        doa[rows_at(((place - s) & 3) * TOK, TOK)] = piece[...]
    for b in range(4):
        pq1[b * 128 : (b + 1) * 128] = qa[where1[b]]
        pq2[b * 64 : (b + 1) * 64] = qa[where2[b]]
    newtop[...] = top[...]

    for valid, tiles in groups:

        @pl.when(valid)
        def _(tiles=tiles):
            highs = []
            for x, _, scores, _, values, _, queries, _ in tiles:
                half = x.shape[0] // 2
                ones_beside(values, x[half:])
                product = dot_nt(queries[...], x[:half]) * SCALE2
                scores[...] = product
                highs.append(wide_max(product))
            for high, (_, _, _, _, _, where, _, _) in zip(highs, tiles):
                size = high.shape[0] // 4
                for b in range(4):
                    part = high[b * size : (b + 1) * size]
                    newtop[where[b]] = jnp.maximum(newtop[where[b]], part)

    shrink = jnp.exp2(top[...] - newtop[...])
    newout[:, :DIM] = out[:, :DIM] * shrink
    newout[:, DIM:] = out[:, DIM:] * shrink

    for valid, tiles in groups:

        @pl.when(valid)
        def _(tiles=tiles):
            sums = []
            for _, _, scores, weights, values, where, _, _ in tiles:
                level = jnp.concatenate([newtop[r][:, :1] for r in where], axis=0)
                w = jnp.exp2(scores[...] - level).astype(BF16)
                weights[...] = w
                sums.append(dot_nn(w, values[...]))
            for total, (_, _, _, _, _, where, _, _) in zip(sums, tiles):
                size = total.shape[0] // 4
                for b in range(4):
                    newout[where[b]] += total[b * size : (b + 1) * size]

    inv[...] = 1.0 / newout[:, DIM:]
    grads = doa[...].astype(F32)
    row_delta = jnp.sum(grads * newout[:, :DIM] * inv[...], axis=1, keepdims=True)
    delta[...] = jnp.broadcast_to(row_delta, delta.shape)
    factor[...] = shrink * inv[...]
    dq[...] = jnp.zeros(dq.shape, F32)
    for b in range(4):
        pd1[b * 128 : (b + 1) * 128] = (doa[where1[b]].astype(F32) * inv[where1[b]]).astype(BF16)
        pd2[b * 64 : (b + 1) * 64] = (doa[where2[b]].astype(F32) * inv[where2[b]]).astype(BF16)

    for valid, tiles in groups:

        @pl.when(valid)
        def _(tiles=tiles):
            parts = []
            for x, g, _, weights, _, where, queries, grad_low in tiles:
                half = x.shape[0] // 2
                prob = dot_nt(grad_low[...], x[half:])
                level = jnp.concatenate([(delta[r] * inv[r])[:, :1] for r in where], axis=0)
                w = weights[...]
                score_grad = (w.astype(F32) * (prob - level)).astype(BF16)
                g[half:] = dot_tn(w, grad_low[...]).astype(BF16)
                g[:half] = (dot_tn(score_grad, queries[...]) * SCALE).astype(BF16)
                parts.append(dot_nn(score_grad, x[:half]))
            for part, (_, _, _, _, _, where, _, _) in zip(parts, tiles):
                size = part.shape[0] // 4
                for b in range(4):
                    dq[where[b]] += part[b * size : (b + 1) * size]


def own_backward_kernel(
    offsets, e0, e1, e2, factor, delta, doa, qa, kv, both, dq_in,
    o0, o1, o2, o3, dkv, dq, low, shift, dkv1, dkv2,
):
    place, _, off1, group2 = places(offsets)
    kv1, kv2 = both.at[:1024], both.at[1024:]
    low[...] = (doa[...].astype(F32) * factor[...]).astype(BF16)
    shift[...] = factor[...] * delta[...]
    dq[...] = dq_in[...]
    for b in range(3, -1, -1):
        strip = slice(b * 256, (b + 1) * 256)
        n0, n1 = (b + 1) * 256, (b + 1) * 128
        rows1 = rows_at(b * 256 + off1 * 128, 128)
        rows2 = rows_at(b * 256 + group2 * 64, 64)
        d1 = slice(b * 128, (b + 1) * 128)
        d2 = slice(b * 64, (b + 1) * 64)
        parts = (
            (strip, strip, e0, kv, BLOCK, n0, dkv),
            (rows1, d1, e1, kv1, 512, n1, dkv1),
            (rows2, d2, e2, kv2, 256, 256, dkv2),
        )
        for rows, part, weights, pair, half, count, grads in parts:
            grad_low = low[rows]
            prob = dot_nt(grad_low, pair[half : half + count])
            w = weights[part, :count]
            score_grad = (w.astype(F32) * (prob - shift[rows][:, :1])).astype(BF16)
            dq[rows] += dot_nn(score_grad, pair[:count])
            key_term = dot_tn(score_grad, qa[rows])
            value_term = dot_tn(w, grad_low)
            if b == 3:
                grads[:count] = key_term
                grads[half : half + count] = value_term
            else:
                grads[:count] += key_term
                grads[half : half + count] += value_term
    for p in range(4):
        for part in range(2):
            dkv[rows_at(part * BLOCK + p * 256 + off1 * 128, 128)] += dkv1[
                part * 512 + p * 128 : part * 512 + (p + 1) * 128
            ]
            dkv[rows_at(part * BLOCK + p * 256 + group2 * 64, 64)] += dkv2[
                part * 256 + p * 64 : part * 256 + (p + 1) * 64
            ]
    for s, target in enumerate((o0, o1, o2, o3)):
        at = ((place + s) & 3) * TOK
        target[:TOK] = (dkv[rows_at(at, TOK)] * SCALE).astype(BF16)
        target[TOK : 2 * TOK] = dkv[rows_at(BLOCK + at, TOK)].astype(BF16)
        target[2 * TOK :] = (dq[rows_at(at, TOK)] * SCALE).astype(BF16)


def combine_kernel(ya, yb, yc, o0, o1, o2, o3):
    place, _ = place_and_block()
    for s, target in enumerate((o0, o1, o2, o3)):
        token = (place + s) & 3
        for part in range(2):
            one = rows_at(part * 512 + token * 128, 128)
            two = part * 256 + token * 64
            target[part * 128 : (part + 1) * 128] = ya[one]
            target[256 + part * 64 : 256 + (part + 1) * 64] = (
                ya[rows_at(1024 + two, 64)].astype(F32)
                + yb[rows_at(two, 64)].astype(F32)
                + yc[rows_at(two, 64)].astype(F32)
            ).astype(BF16)


def finish_own_kernel(p0, p1, p2, p3, dq, dk, dv, held):
    place, block = place_and_block()
    for s, piece in enumerate((p0, p1, p2, p3)):
        cols = cols_at(head_at((place - s) & 3, block))
        dk[:, cols] = piece[:TOK].astype(F32)
        dv[:, cols] = piece[TOK : 2 * TOK].astype(F32)
        held[:, cols] = piece[2 * TOK :]
    dq[...] = dot_nn(unsort_matrix(), held[...]).astype(BF16)


def finish_kernel(offsets, in_k, in_v, c0, c1, c2, c3, dk, dv, total, low_k, low_v, sem):
    place, block = place_and_block()
    unsort = unsort_matrix()
    copies = []
    for part, (own, low, out) in enumerate(((in_k, low_k, dk), (in_v, low_v, dv))):
        total[part] = own[...]
        for s, cross in enumerate((c0, c1, c2, c3)):
            head = head_at((place - s) & 3, block)
            off1, off2 = offsets[head, 1], offsets[head, 2]
            group2 = ((off2 & 1) << 1) | (off2 >> 1)
            cols = cols_at(head)
            rows1, rows2 = rows_at(off1 * 128, 128), rows_at(group2 * 64, 64)
            sums = total.at[part]
            sums[rows1, cols] += cross[part * 128 : (part + 1) * 128].astype(F32)
            sums[rows2, cols] += cross[256 + part * 64 : 256 + (part + 1) * 64].astype(F32)
        low[...] = dot_nn(unsort, total[part].astype(BF16)).astype(BF16)
        copies.append(pltpu.make_async_copy(low, out, sem.at[part]))
        copies[part].start()
    for copy in copies:
        copy.wait()


def local(queries, keys, values, out_grad, w_out, offsets):
    devices = lax.axis_size("ctx")

    def at(index):
        return (index + 2) % devices

    def exchange(part, s, blocks=(0, 1, 2, 3)):
        route = [
            (at(u), at(u // 4 * 4 + (u % 4 + s) % 4))
            for u in range(devices)
            if u // 4 % 4 in blocks
        ]
        return lax.ppermute(part, "ctx", route)

    def to_blocks(part, pairs, back=False):
        route = []
        for first in range(0, devices, 16):
            for source, target in pairs:
                for place in range(4):
                    there = 3 - place if (source + target) % 2 else place
                    pair = (at(first + 4 * source + place), at(first + 4 * target + there))
                    route.append(pair[::-1] if back else pair)
        return lax.ppermute(part, "ctx", route)

    def across(part, m):
        return lax.ppermute(part, "tp", [(i, i ^ m) for i in range(4)])

    def after(part, *others):
        return lax.optimization_barrier((part, *others))[0]

    links = (((0, 1), (2, 3)), ((1, 2), (0, 3)), ((0, 2), (1, 3)))
    width = out_grad.shape[1]
    half = (2, 4 * DIM, width)

    grad_y = across(out_grad, 2)
    packed = call(
        pack_kernel,
        [((3 * TOK, DIM), BF16)] * 4,
        [pltpu.VMEM((3, TOK, 4 * DIM), BF16), pltpu.SemaphoreType.DMA((3,))],
        name="pack",
        flops=2 * 10**8,
        bytes_accessed=2 << 20,
        far=(0, 1, 2),
    )(queries, keys, values)
    pieces = [exchange(packed[s], s) for s in (1, 2, 3)]
    grad_core = across(after(out_grad, packed[1]), 1)
    near, w_far = call(
        grad_near_kernel,
        [((TOK, 4 * DIM), F32), (half, BF16)],
        [pltpu.VMEM(half, BF16), pltpu.SemaphoreType.DMA((4,))],
        name="grad_near",
        far=(2,),
    )(out_grad, grad_core, w_out)
    grad_far = across(after(grad_y, near, *pieces), 1)
    grads = call(
        grad_far_kernel,
        [((TOK, DIM), BF16)] * 4,
        [pltpu.VMEM((TOK, 4 * DIM), BF16)],
        name="grad_far",
        flops=TOK * 512 * 4096,
        bytes_accessed=4 << 20,
    )(near, grad_y, grad_far, w_far)

    qa, kv, both, kv2 = call(
        gather_kernel,
        [
            ((BLOCK, DIM), BF16),
            ((2 * BLOCK, DIM), BF16),
            ((1536, DIM), BF16),
            ((512, DIM), BF16),
        ],
        name="gather",
        flops=10**7,
        bytes_accessed=2 << 20,
    )(offsets, packed[0], after(pieces[0], near), *pieces[1:])
    first, rest = after(both, grads[1]), after(kv2, grads[1])
    xs = [to_blocks(part, pairs) for part, pairs in zip((first, rest, rest), links)]
    grad_parts = [grads[0]] + [exchange(grads[s], s) for s in (1, 2, 3)]

    e0, e1, e2, top, out = call(
        own_forward_kernel,
        [
            ((BLOCK, BLOCK), BF16),
            ((512, 512), BF16),
            ((256, 256), BF16),
            ((BLOCK, DIM), F32),
            ((BLOCK, 2 * DIM), F32),
        ],
        [
            pltpu.VMEM((BLOCK, 2 * DIM), BF16),
            pltpu.VMEM((512, 2 * DIM), BF16),
            pltpu.VMEM((256, 2 * DIM), BF16),
        ],
        name="own_forward",
        flops=10**9,
        bytes_accessed=6 << 20,
    )(offsets, qa, kv, both)

    doa, dq, factor, delta, *partials = call(
        cross_kernel,
        [
            ((BLOCK, DIM), BF16),
            ((BLOCK, DIM), F32),
            ((BLOCK, DIM), F32),
            ((BLOCK, DIM), F32),
            ((1536, DIM), BF16),
            ((512, DIM), BF16),
            ((512, DIM), BF16),
        ],
        [
            pltpu.VMEM((512, DIM), BF16),
            pltpu.VMEM((256, DIM), BF16),
            pltpu.VMEM((512, DIM), BF16),
            pltpu.VMEM((256, DIM), BF16),
            pltpu.VMEM((512, 512), F32),
            pltpu.VMEM((3, 256, 256), F32),
            pltpu.VMEM((512, 512), BF16),
            pltpu.VMEM((3, 256, 256), BF16),
            pltpu.VMEM((BLOCK, DIM), F32),
            pltpu.VMEM((BLOCK, 2 * DIM), F32),
            pltpu.VMEM((BLOCK, DIM), F32),
            pltpu.VMEM((512, 2 * DIM), BF16),
            pltpu.VMEM((3, 256, 2 * DIM), BF16),
        ],
        name="cross",
        flops=10**9,
        bytes_accessed=6 << 20,
    )(offsets, qa, *xs, top, out, *grad_parts)
    ys = [to_blocks(part, pairs, back=True) for part, pairs in zip(partials, links)]

    own_parts = call(
        own_backward_kernel,
        [((3 * TOK, DIM), BF16)] * 4,
        [
            pltpu.VMEM((2 * BLOCK, DIM), F32),
            pltpu.VMEM((BLOCK, DIM), F32),
            pltpu.VMEM((BLOCK, DIM), BF16),
            pltpu.VMEM((BLOCK, DIM), F32),
            pltpu.VMEM((1024, DIM), F32),
            pltpu.VMEM((512, DIM), F32),
        ],
        name="own_backward",
        flops=2 * 10**9,
        bytes_accessed=8 << 20,
    )(offsets, e0, e1, e2, factor, delta, doa, qa, kv, both, dq)
    own_parts = list(own_parts)
    own_parts[3] = after(own_parts[3], *ys[1:])
    own_parts = [own_parts[0]] + [exchange(own_parts[s], s) for s in (1, 2, 3)]

    cross_parts = call(
        combine_kernel,
        [((384, DIM), BF16)] * 4,
        name="combine",
        flops=10**7,
        bytes_accessed=1 << 20,
    )(after(ys[0], own_parts[1]), *ys[1:])
    cross_parts = [cross_parts[0]] + [
        exchange(cross_parts[s], s, (0, 1, 2)) for s in (1, 2, 3)
    ]
    wide = (TOK, 4 * DIM)
    query_grad, own_k, own_v = call(
        finish_own_kernel,
        [(wide, BF16), (wide, F32), (wide, F32)],
        [pltpu.VMEM(wide, BF16)],
        name="finish_own",
    )(*own_parts)
    cross_parts[1] = after(cross_parts[1], query_grad)
    key_value_grads = call(
        finish_kernel,
        [(wide, BF16)] * 2,
        [
            pltpu.VMEM((2, *wide), F32),
            pltpu.VMEM(wide, BF16),
            pltpu.VMEM(wide, BF16),
            pltpu.SemaphoreType.DMA((2,)),
        ],
        name="finish",
        outs_far=True,
    )(
        offsets, own_k, own_v, *cross_parts
    )
    return (query_grad, *key_value_grads)


def solution(mesh):
    return jax.shard_map(
        local,
        mesh=mesh,
        in_specs=(
            P("ctx", "tp"),
            P("ctx", "tp"),
            P("ctx", "tp"),
            P("ctx", "tp"),
            P("tp", None),
            P("tp", None),
        ),
        out_specs=(P("ctx", "tp"), P("ctx", "tp"), P("ctx", "tp")),
        check_vma=False,
    )
```
